128 devices in a mesh: row: 8 (over x, core), col: 16 (over z, y).
Axes of the slice: x: 4, y: 4, z: 4, core: 2. Of those that a mesh axis runs over, the one named last changes fastest.
Arguments:
- rhs: float32 [65536, 1024], P('col', 'row'), may hold values from -6 to 6
- factors: bfloat16 [65536, 2048], P('col', 'row'), may hold values from -0.15625 to 0.15625
- diag_inv: float32 [4, 512, 512], replicated, may hold values from -2 to 2, as said below
Outputs:
- solution: float32 [65536, 1024], P('col', 'row')
The draws below stay inside these ranges and needn't reach their ends.
Inputs may be any that keep to these rules, and one draw needn't show every extreme that they name: `diag_inv`: entries off the diagonal of each block lie within 2 / sqrt(512) in magnitude; diagonal entries lie in 0.5 to 2.
All inputs are finite; a program needn't handle non-finite values.
Results may differ from the reference program's by a relative error of at most 0.0038.
Values may be sent and summed in bfloat16 or wider, within the bound.
No kernel may reach another device: no remote copies, remote signals or barrier semaphores. Data moves between devices by JAX's collectives and lax.ppermute only.
A program may use at most 128 MiB of HBM per device.

```python
import jax
import jax.numpy as jnp
from jax import lax

NB = 512
STEPS = 4
NW = 2048
ROWS = 65536
SPAN = 16384
RHS = 1024


def draw_diag_inv(key, part):
    base = jax.random.fold_in(key, 7)
    key_low, key_up, key_dia = jax.random.split(base, 3)
    scale = 0.5 / jnp.sqrt(jnp.float32(NB))
    lower_part = jnp.clip(jax.random.normal(key_low, (STEPS, NB, NB), jnp.float32), -4.0, 4.0) * scale
    upper_part = jnp.clip(jax.random.normal(key_up, (STEPS, NB, NB), jnp.float32), -4.0, 4.0) * scale
    diagonal = jnp.exp(jax.random.uniform(key_dia, (STEPS, NB), jnp.float32, jnp.log(0.5), jnp.log(2.0)))
    index = jnp.arange(NB)
    below = index[:, None] > index[None, :]
    above = index[:, None] < index[None, :]
    packed = jnp.where(below[None], lower_part, jnp.where(above[None], upper_part, 0.0))
    return (packed + diagonal[:, :, None] * jnp.eye(NB, dtype=jnp.float32)[None]).astype(jnp.float32)


def block_levels(own_key, shape, cuts, smallest, high):
    loudness = 1.0
    for dim, blocks in cuts:
        draws = jax.random.uniform(jax.random.fold_in(jax.random.fold_in(own_key, 6), dim), (blocks,), jnp.float32, smallest / len(cuts), high / len(cuts))
        loudness = loudness * jnp.repeat(jnp.exp(draws), shape[dim] // blocks).reshape((-1,) + (1,) * (len(shape) - 1 - dim))
    return loudness


def gaussian(rng, extent, scale, most, shards=(), held_as=jnp.bfloat16):
    factor_of = block_levels(rng, extent, shards, -0.22, 0.18) if shards else 1.0
    values = jax.random.normal(rng, extent, jnp.float32) * scale * factor_of
    return jnp.minimum(jnp.maximum(values, -most), most).astype(held_as)


def setup_inputs(seed: int = 0) -> dict:
    arg_keys = jax.random.split(jax.random.key(seed), 4)
    rhs = gaussian(arg_keys[0], (ROWS, RHS), 1.0, 6.0, ((0, 16), (1, 8)), jnp.float32)
    factors = gaussian(arg_keys[1], (ROWS, NW), (16 * NW // 25) ** -0.5, 0.15625, ((0, 16), (1, 8)))
    diag_inv = draw_diag_inv(jax.random.fold_in(arg_keys[3], 71), 0)
    return dict(rhs=rhs, factors=factors, diag_inv=diag_inv)


def reference(rhs, factors, diag_inv):
    index = jnp.arange(NB)
    strict_lower = index[:, None] > index[None, :]
    eye = jnp.eye(NB, dtype=jnp.float32)
    work = rhs.astype(jnp.float32)
    for step in range(STEPS):
        lower_inv = jnp.where(strict_lower, diag_inv[step], jnp.float32(0.0)) + eye
        first = step * SPAN
        solved = jnp.dot(lower_inv, work[first:first + NB], precision=lax.Precision.HIGHEST, preferred_element_type=jnp.float32)
        work = work.at[first:first + NB].set(solved)
        below = first + NB
        if below < ROWS:
            product = jnp.dot(factors[below:, step * NB:(step + 1) * NB], solved.astype(jnp.bfloat16), preferred_element_type=jnp.float32)
            work = work.at[below:].add(-product)
    for step in reversed(range(STEPS)):
        upper_inv = jnp.triu(diag_inv[step])
        first = step * SPAN
        solved = jnp.dot(upper_inv, work[first:first + NB], precision=lax.Precision.HIGHEST, preferred_element_type=jnp.float32)
        work = work.at[first:first + NB].set(solved)
        if first > 0:
            product = jnp.dot(factors[:first, step * NB:(step + 1) * NB], solved.astype(jnp.bfloat16), preferred_element_type=jnp.float32)
            work = work.at[:first].add(-product)
    return work
```

```python
import functools

import jax
import jax.numpy as jnp
from jax import lax
from jax.experimental import pallas as pl
from jax.experimental.pallas import tpu as pltpu
from jax.sharding import PartitionSpec as P

NX, NH, NZ, NY = 4, 2, 4, 4
NB = 512
HB = 256
F32, BF16 = jnp.float32, jnp.bfloat16


def pairs(move):
    out = []
    for r in range(NX * NH):
        for c in range(NZ * NY):
            x, h = divmod(r, NH)
            z, y = divmod(c, NY)
            to = move(x, h, z, y)
            if to is not None:
                x2, h2, z2, y2 = to
                out.append((r * NZ * NY + c, ((x2 % NX) * NH + h2 % NH) * NZ * NY + (z2 % NZ) * NY + y2 % NY))
    return out


def send(value, move):
    return lax.ppermute(value, ("row", "col"), pairs(move))


def x_plus(x, h, z, y):
    return (x + 1, h, z, y)


def x_minus(x, h, z, y):
    return (x - 1, h, z, y)


def other_core(x, h, z, y):
    return (x, 1 - h, z, y)


def z_move(src, dst):
    return lambda x, h, z, y: (x, h, dst, y) if (y == 0 and z == src) else None


def y_move(step):
    return lambda x, h, z, y: (x, h, z, step) if y == 0 else None


def dot(a, b):
    return jnp.dot(a, b, preferred_element_type=F32)


def split(a):
    hi = a.astype(BF16)
    return hi, (a - hi.astype(F32)).astype(BF16)


def tri_dot(matrix, v):
    mh, ml = split(matrix)
    vh, vl = split(v)
    return dot(mh, vh) + (dot(mh, vl) + dot(ml, vh))


def lower_mask(d):
    i = lax.broadcasted_iota(jnp.int32, d.shape, 0)
    j = lax.broadcasted_iota(jnp.int32, d.shape, 1)
    return jnp.where(i > j, d, 0.0)


def upper_mask(d):
    i = lax.broadcasted_iota(jnp.int32, d.shape, 0)
    j = lax.broadcasted_iota(jnp.int32, d.shape, 1)
    return jnp.where(i <= j, d, 0.0)


def start_kernel(ids, b_ref, d_ref, y_ref, yb_ref):
    w = b_ref[...]
    y = w + tri_dot(lower_mask(d_ref[0]), w)
    y_ref[...] = y
    yb_ref[...] = y.astype(BF16)


def block_product(ids, blocks, j, v_ref, acc_ref):
    x, h = ids[0], ids[1]
    for d in range(NX):
        @pl.when(lax.rem(x + d, NX) == j)
        def _():
            same, other = blocks[2 * d], blocks[2 * d + 1]
            acc_ref[...] -= dot(same[...], v_ref[pl.ds(pl.multiple_of(h * HB, HB), HB), :]) + dot(
                other[...], v_ref[pl.ds(pl.multiple_of((1 - h) * HB, HB), HB), :]
            )


def forward_kernel(j, ids, w_ref, v_ref, d_ref, *rest):
    blocks, (w_out, y_ref, yb_ref) = rest[:8], rest[8:]
    w_out[...] = w_ref[...]
    block_product(ids, blocks, j, v_ref, w_out)
    w = w_out[...]
    y = w + tri_dot(lower_mask(d_ref[0]), w)
    y_ref[...] = y
    yb_ref[...] = y.astype(BF16)


def turn_kernel(ids, w_ref, y1_ref, y2_ref, d_ref, p_same, p_other, *rest):
    blocks, (y_ref, yb_ref, x_ref, acc) = rest[:8], rest[8:]
    h = ids[1]
    acc[...] = w_ref[...]
    block_product(ids, blocks, 2, y2_ref, acc)
    w = acc[...]
    y3 = w + tri_dot(lower_mask(d_ref[3]), w)
    y_ref[...] = y3
    yb_ref[...] = y3.astype(BF16)

    def prefetched(slot, row):
        cols = slice(slot * HB, (slot + 1) * HB)
        return dot(p_same[:, cols], x_ref[pl.ds(pl.multiple_of(row + h * HB, HB), HB), :]) + dot(
            p_other[:, cols], x_ref[pl.ds(pl.multiple_of(row + (1 - h) * HB, HB), HB), :]
        )

    x_ref[2 * NB : 3 * NB, :] = tri_dot(upper_mask(d_ref[3]), y3).astype(BF16)
    t = y2_ref[...].astype(F32) - prefetched(0, 2 * NB)
    x_ref[NB : 2 * NB, :] = tri_dot(upper_mask(d_ref[2]), t).astype(BF16)
    t = y1_ref[...].astype(F32) - prefetched(1, NB) - prefetched(2, 2 * NB)
    x_ref[0:NB, :] = tri_dot(upper_mask(d_ref[1]), t).astype(BF16)


def window_kernel(ids, out_in, y_ref, v0_ref, v_ref, d_ref, *rest):
    blocks, (out_ref, acc) = rest[:8], rest[8:]
    x, h, z, owner = ids[0], ids[1], ids[2], ids[3] == 0
    acc[...] = jnp.where(owner, y_ref[...], out_in[...])
    for d in range(NX):
        j = lax.rem(x + d, NX)
        for s in range(2):
            part = h if s == 0 else 1 - h

            @pl.when(jnp.logical_and(j == 0, jnp.logical_not(owner)))
            def _():
                acc[...] -= dot(blocks[2 * d + s][...], v0_ref[pl.ds(pl.multiple_of(part * HB, HB), HB), :])

            @pl.when(jnp.logical_and(j > 0, jnp.logical_or(jnp.logical_not(owner), j > z)))
            def _():
                acc[...] -= dot(
                    blocks[2 * d + s][...], v_ref[pl.ds(pl.multiple_of((j - 1) * NB + part * HB, HB), HB), :]
                )

    @pl.when(owner)
    def _():
        out_ref[...] = tri_dot(upper_mask(d_ref[0]), acc[...])

    @pl.when(jnp.logical_not(owner))
    def _():
        out_ref[...] = acc[...]


def rows_kernel(ids, out_in, v_ref, *rest):
    blocks, out_ref = rest[:8], rest[8]
    x, h = ids[0], ids[1]
    acc = out_in[...]
    for d in range(NX):
        j = lax.rem(x + d, NX)
        for s in range(2):
            part = h if s == 0 else 1 - h
            acc -= dot(blocks[2 * d + s][...], v_ref[pl.ds(pl.multiple_of(j * NB + part * HB, HB), HB), :])
    out_ref[...] = acc


def whole(shape):
    return pl.BlockSpec(shape, lambda i, ids: (0,) * len(shape))


def diag_spec():
    return pl.BlockSpec((1, NB, NB), lambda i, ids: (ids[2], 0, 0))


def call(kernel, ids, args, specs, outs, out_specs, scratch=(), grid=(1,), aliases={}, flops=0):
    moved = sum(a.size * a.dtype.itemsize for a in args)
    return pl.pallas_call(
        kernel,
        grid_spec=pltpu.PrefetchScalarGridSpec(
            num_scalar_prefetch=1, grid=grid, in_specs=specs, out_specs=out_specs, scratch_shapes=scratch
        ),
        out_shape=outs,
        input_output_aliases=aliases,
        cost_estimate=pl.CostEstimate(flops=flops, bytes_accessed=moved, transcendentals=0),
        compiler_params=pltpu.CompilerParams(vmem_limit_bytes=48 * 1024 * 1024),
    )(ids, *args)


def ring(own):
    half = own.shape[0] // 2
    before = send(own, x_plus)
    after = send(own, x_minus)
    top = send(before[:half], x_plus)
    bottom = send(after[half:], x_minus)
    return before, after, top, bottom


def body(rhs, factors, diag_inv):
    rows, cols = rhs.shape
    r, c = lax.axis_index("row"), lax.axis_index("col")
    x, h, z, y = r // NH, r % NH, c // NY, c % NY
    ids = jnp.stack([x, h, z, y]).astype(jnp.int32)
    owner = y == 0
    vec = jax.ShapeDtypeStruct((NB, cols), F32)
    vecb = jax.ShapeDtypeStruct((NB, cols), BF16)
    vspec = whole((NB, cols))

    own0, own1 = factors[:NB], factors[NB:]
    before0, after0, top0, bottom0 = ring(own0)
    far0 = jnp.concatenate([top0, bottom0], axis=0)
    same0 = [own0, after0, far0, before0]
    window = [b for s in same0 for b in (s, send(s, other_core))]
    before1, after1, top1, bottom1 = ring(own1)
    o1, a1, b1, t1, u1 = (send(v, other_core) for v in (own1, after1, before1, top1, bottom1))

    wspecs = [whole((NB, HB))] * 8
    base = rhs[:NB]
    flops = 2 * NB * NB * cols * 4
    y_z0, yb = call(start_kernel, ids, (base, diag_inv), [vspec, diag_spec()], (vec, vecb), (vspec, vspec), flops=flops)
    moves = [send(yb, z_move(0, t)) for t in (1, 2, 3)]
    y0 = jnp.where(z == 0, yb, moves[0] + moves[1] + moves[2])
    early = [send(y0, y_move(t)) for t in (1, 2, 3)]
    v0 = jnp.where(owner, y0, early[0] + early[1] + early[2])

    def forward(j, w, v):
        return call(
            functools.partial(forward_kernel, j), ids, (w, v, diag_inv, *window),
            [vspec, vspec, diag_spec(), *wspecs], (vec, vec, vecb), (vspec, vspec, vspec), flops=2 * flops,
        )

    w, y_z1, yb = forward(0, base, y0)
    moves = [send(yb, z_move(1, t)) for t in (2, 3)]
    y1 = jnp.where(z == 1, yb, moves[0] + moves[1])
    w, y_z2, yb = forward(1, w, y1)
    y2_in = send(yb, z_move(2, 3))
    y2 = jnp.where(z == 2, yb, y2_in)

    def pick(j):
        d = (j - x + NX) % NX
        return jnp.where(d == 0, same0[0], jnp.where(d == 1, same0[1], jnp.where(d == 2, same0[2], same0[3])))

    p23 = send(pick(3), z_move(2, 3))
    p1 = send(jnp.concatenate([pick(2), pick(3)], axis=1), z_move(1, 3))
    p_same = jnp.concatenate([p23, p1], axis=1)
    p_other = send(p_same, other_core)

    pspec = whole((NB, 3 * HB))
    y_z3, yb3, xs = call(
        turn_kernel, ids, (w, y1, y2, diag_inv, p_same, p_other, *window),
        [vspec, vspec, vspec, whole((4, NB, NB)), pspec, pspec, *wspecs],
        (vec, vecb, jax.ShapeDtypeStruct((3 * NB, cols), BF16)), (vspec, vspec, whole((3 * NB, cols))),
        scratch=[pltpu.VMEM((NB, cols), F32)], flops=6 * flops,
    )
    to0 = send(xs, z_move(3, 0))
    to1 = send(xs[NB:], z_move(3, 1))
    to2 = send(xs[2 * NB :], z_move(3, 2))
    x1 = to0[:NB]
    x2 = to0[NB : 2 * NB] + to1[:NB]
    x3 = to0[2 * NB :] + to1[NB:] + to2
    late = jnp.concatenate(
        [jnp.where(z >= 1, y1, x1), jnp.where(z >= 2, y2, x2), jnp.where(z >= 3, yb3, x3)], axis=0
    )
    spread = [send(late, y_move(t)) for t in (1, 2, 3)]
    v = jnp.where(owner, late, spread[0] + spread[1] + spread[2])
    y_own = jnp.where(z == 0, y_z0, jnp.where(z == 1, y_z1, jnp.where(z == 2, y_z2, y_z3)))

    rest = rows - NB
    tile = 256
    half_tiles = rest // 2 // tile
    v_all = jnp.concatenate([v0, v], axis=0)
    out = rhs
    for first, far, far_other in ((0, top1, t1), (half_tiles, bottom1, u1)):
        near = pl.BlockSpec((tile, HB), lambda i, ids, first=first: (first + i, 0))
        local = pl.BlockSpec((tile, HB), lambda i, ids: (i, 0))
        ospec = pl.BlockSpec((tile, cols), lambda i, ids, first=first: (NB // tile + first + i, 0))
        out = call(
            rows_kernel, ids, (out, v_all, own1, o1, after1, a1, far, far_other, before1, b1),
            [ospec, whole((4 * NB, cols)), near, near, near, near, local, local, near, near],
            jax.ShapeDtypeStruct(out.shape, F32), ospec, grid=(half_tiles,), aliases={1: 0}, flops=rest * 4 * NB * cols,
        )
    ospec = pl.BlockSpec((NB, cols), lambda i, ids: (0, 0))
    return call(
        window_kernel, ids, (out, y_own, v0, v, diag_inv, *window),
        [ospec, vspec, vspec, whole((3 * NB, cols)), diag_spec(), *wspecs],
        jax.ShapeDtypeStruct(out.shape, F32), ospec, scratch=[pltpu.VMEM((NB, cols), F32)], aliases={1: 0},
        flops=2 * flops,
    )


def solution(mesh):
    placed = (P("col", "row"), P("col", "row"), P())
    return jax.shard_map(body, mesh=mesh, in_specs=placed, out_specs=P("col", "row"), check_vma=False)
```

```python
import functools

import jax
import jax.numpy as jnp
from jax import lax
from jax.experimental import pallas as pl
from jax.experimental.pallas import tpu as pltpu
from jax.sharding import PartitionSpec as P

NX, NH, NZ, NY = 4, 2, 4, 4
NB = 512
HB = 256
F32, BF16 = jnp.float32, jnp.bfloat16


def pairs(move):
    out = []
    for r in range(NX * NH):
        for c in range(NZ * NY):
            x, h = divmod(r, NH)
            z, y = divmod(c, NY)
            to = move(x, h, z, y)
            if to is not None:
                x2, h2, z2, y2 = to
                out.append((r * NZ * NY + c, ((x2 % NX) * NH + h2 % NH) * NZ * NY + (z2 % NZ) * NY + y2 % NY))
    return out


def send(value, move):
    return lax.ppermute(value, ("row", "col"), pairs(move))


def x_plus(x, h, z, y):
    return (x + 1, h, z, y)


def x_minus(x, h, z, y):
    return (x - 1, h, z, y)


def x_far(x, h, z, y):
    return (x + 2, h, z, y)


def other_core(x, h, z, y):
    return (x, 1 - h, z, y)


def z_move(src, dst):
    return lambda x, h, z, y: (x, h, dst, y) if (y == 0 and z == src) else None


def y_move(step):
    return lambda x, h, z, y: (x, h, z, step) if y == 0 else None


def dot(a, b):
    return jnp.dot(a, b, preferred_element_type=F32)


def split(a):
    hi = a.astype(BF16)
    return hi, (a - hi.astype(F32)).astype(BF16)


def apply(hi_ref, lo_ref, v):
    vh, vl = split(v)
    return dot(hi_ref[...], vh) + (dot(hi_ref[...], vl) + dot(lo_ref[...], vh))


def lower_mask(d):
    i = lax.broadcasted_iota(jnp.int32, d.shape, 0)
    j = lax.broadcasted_iota(jnp.int32, d.shape, 1)
    return jnp.where(i > j, d, 0.0)


def upper_mask(d):
    i = lax.broadcasted_iota(jnp.int32, d.shape, 0)
    j = lax.broadcasted_iota(jnp.int32, d.shape, 1)
    return jnp.where(i <= j, d, 0.0)


def start_kernel(ids, b_ref, d_ref, y_ref, yb_ref, lh_ref, ll_ref):
    lh_ref[...], ll_ref[...] = split(lower_mask(d_ref[0]))
    w = b_ref[...]
    y = w + apply(lh_ref, ll_ref, w)
    y_ref[...] = y
    yb_ref[...] = y.astype(BF16)


def upper_kernel(ids, d_ref, *out):
    for n, j in enumerate((ids[2], 1, 2)):
        out[2 * n][...], out[2 * n + 1][...] = split(upper_mask(d_ref[j]))


def block_product(ids, blocks, j, v_ref, acc_ref):
    x, h = ids[0], ids[1]
    for d in range(NX):
        @pl.when(lax.rem(x + d, NX) == j)
        def _():
            same, other = blocks[2 * d], blocks[2 * d + 1]
            acc_ref[...] -= dot(same[...], v_ref[pl.ds(pl.multiple_of(h * HB, HB), HB), :]) + dot(
                other[...], v_ref[pl.ds(pl.multiple_of((1 - h) * HB, HB), HB), :]
            )


def gather_own(ids, j, v_ref, own_ref, received):
    total = received[0][...]
    for piece in received[1:]:
        total = total + piece[...]
    v_ref[...] = jnp.where(ids[2] == j, own_ref[...], total)


def forward_kernel(j, count, ids, w_ref, own_ref, lh_ref, ll_ref, *rest):
    received, blocks = rest[:count], rest[count : count + 8]
    v_ref, w_out, y_ref, yb_ref = rest[count + 8 :]
    gather_own(ids, j, v_ref, own_ref, received)
    w_out[...] = w_ref[...]
    block_product(ids, blocks, j, v_ref, w_out)
    w = w_out[...]
    y = w + apply(lh_ref, ll_ref, w)
    y_ref[...] = y
    yb_ref[...] = y.astype(BF16)


def turn_kernel(ids, w_ref, y1_ref, own_ref, y2_in, lh, ll, uzh, uzl, u1h, u1l, u2h, u2l, p_same, p_other, *rest):
    blocks, (y2_ref, y_ref, yb_ref, x_ref, x23_ref, x3_ref, acc) = rest[:8], rest[-7:]
    h = ids[1]
    gather_own(ids, 2, y2_ref, own_ref, [y2_in])
    acc[...] = w_ref[...]
    block_product(ids, blocks, 2, y2_ref, acc)
    w = acc[...]
    y3 = w + apply(lh, ll, w)
    y_ref[...] = y3
    yb_ref[...] = y3.astype(BF16)

    def prefetched(slot, row):
        cols = slice(slot * HB, (slot + 1) * HB)
        return dot(p_same[:, cols], x_ref[pl.ds(pl.multiple_of(row + h * HB, HB), HB), :]) + dot(
            p_other[:, cols], x_ref[pl.ds(pl.multiple_of(row + (1 - h) * HB, HB), HB), :]
        )

    x3 = apply(uzh, uzl, y3).astype(BF16)
    x_ref[2 * NB : 3 * NB, :] = x3
    x23_ref[NB : 2 * NB, :] = x3
    x3_ref[...] = x3
    t = y2_ref[...].astype(F32) - prefetched(0, 2 * NB)
    x2 = apply(u2h, u2l, t).astype(BF16)
    x_ref[NB : 2 * NB, :] = x2
    x23_ref[0:NB, :] = x2
    t = y1_ref[...].astype(F32) - prefetched(1, NB) - prefetched(2, 2 * NB)
    x_ref[0:NB, :] = apply(u1h, u1l, t).astype(BF16)


def window_kernel(ids, out_in, b_ref, y_ref, v0_ref, v_ref, uh_ref, ul_ref, *rest):
    blocks, (out_ref, acc) = rest[:8], rest[8:]
    x, h, z, owner = ids[0], ids[1], ids[2], ids[3] == 0
    acc[...] = jnp.where(owner, y_ref[...], b_ref[...])
    for d in range(NX):
        j = lax.rem(x + d, NX)
        for s in range(2):
            part = h if s == 0 else 1 - h

            @pl.when(jnp.logical_and(j == 0, jnp.logical_not(owner)))
            def _():
                acc[...] -= dot(blocks[2 * d + s][...], v0_ref[pl.ds(pl.multiple_of(part * HB, HB), HB), :])

            @pl.when(jnp.logical_and(j > 0, jnp.logical_or(jnp.logical_not(owner), j > z)))
            def _():
                acc[...] -= dot(
                    blocks[2 * d + s][...], v_ref[pl.ds(pl.multiple_of((j - 1) * NB + part * HB, HB), HB), :]
                )

    @pl.when(owner)
    def _():
        out_ref[...] = apply(uh_ref, ul_ref, acc[...])

    @pl.when(jnp.logical_not(owner))
    def _():
        out_ref[...] = acc[...]


def rows_of(ids, d, s, v_ref):
    part = ids[1] if s == 0 else 1 - ids[1]
    return v_ref[pl.ds(pl.multiple_of(lax.rem(ids[0] + d, NX) * NB + part * HB, HB), HB), :]


def rows_kernel(distances, aliased, ids, b_ref, v_ref, *rest):
    rest = rest[1:] if aliased else rest
    out_ref = rest[-1]
    acc = b_ref[...]
    for n, d in enumerate(distances):
        for s in range(2):
            acc -= dot(rest[2 * n + s][...], rows_of(ids, d, s, v_ref))
    out_ref[...] = acc
    if len(rest) > 2 * len(distances) + 1:
        pair = rest[2 * len(distances) : -1]
        for t in range(2):
            @pl.when(pl.program_id(0) == t)
            def _():
                for s in range(2):
                    out_ref[...] -= dot(pair[2 * t + s][...], rows_of(ids, 2, s, v_ref))


def late_kernel(ids, to0, to1, to2, y1, y2, y3, *rest):
    late_ref, z = rest[-1], ids[2]
    late_ref[0:NB, :] = jnp.where(z >= 1, y1[...], to0[0:NB, :])
    late_ref[NB : 2 * NB, :] = jnp.where(z >= 2, y2[...], to0[NB : 2 * NB, :] + to1[0:NB, :])
    late_ref[2 * NB :, :] = jnp.where(z >= 3, y3[...], to0[2 * NB :, :] + to1[NB:, :] + to2[...])


def whole(shape):
    return pl.BlockSpec(shape, lambda i, ids: (0,) * len(shape))


ANY = pl.BlockSpec(memory_space=pl.ANY)


def call(kernel, ids, args, specs, outs, out_specs, scratch=(), grid=(1,), aliases={}, limit=14):
    return pl.pallas_call(
        kernel,
        grid_spec=pltpu.PrefetchScalarGridSpec(
            num_scalar_prefetch=1, grid=grid, in_specs=specs, out_specs=out_specs, scratch_shapes=scratch
        ),
        out_shape=outs,
        input_output_aliases=aliases,
        cost_estimate=pl.CostEstimate(flops=1, bytes_accessed=1, transcendentals=0),
        compiler_params=pltpu.CompilerParams(vmem_limit_bytes=limit * 1024 * 1024),
    )(ids, *args)


def ring(own):
    half = own.shape[0] // 2
    before = send(own, x_plus)
    after = send(own, x_minus)
    top = send(before[:half], x_plus)
    bottom = send(after[half:], x_minus)
    return before, after, top, bottom


def body(rhs, factors, diag_inv):
    rows, cols = rhs.shape
    r, c = lax.axis_index("row"), lax.axis_index("col")
    x, h, z, y = r // NH, r % NH, c // NY, c % NY
    ids = jnp.stack([x, h, z, y]).astype(jnp.int32)
    owner = y == 0
    vec = jax.ShapeDtypeStruct((NB, cols), F32)
    vecb = jax.ShapeDtypeStruct((NB, cols), BF16)
    vspec = whole((NB, cols))

    own0 = factors[:NB]
    near0, behind0, far0 = send(own0, x_minus), send(own0, x_plus), send(own0, x_far)
    part = (rows - NB) // 2
    own1, own2 = factors[NB : NB + part], factors[NB + part :]
    before1, after1, top1, bottom1 = ring(own1)
    before2, after2, top2, bottom2 = ring(own2)
    same0 = [own0, near0, far0, behind0]
    window = [b for s in same0 for b in (s, send(s, other_core))]
    o1, a1, b1, t1, u1 = (send(v, other_core) for v in (own1, after1, before1, top1, bottom1))
    o2, a2, b2, t2, u2 = (send(v, other_core) for v in (own2, after2, before2, top2, bottom2))

    wspecs = [whole((NB, HB))] * 8
    mat = jax.ShapeDtypeStruct((NB, NB), BF16)
    mspec = whole((NB, NB))
    first = pl.BlockSpec((NB, cols), lambda i, ids: (0, 0))
    y_z0, yb, lh, ll = call(
        start_kernel, ids, (rhs, diag_inv), [first, pl.BlockSpec((1, NB, NB), lambda i, ids: (ids[2], 0, 0))],
        (vec, vecb, mat, mat), (vspec, vspec, mspec, mspec),
    )
    moves = [send(yb, z_move(0, t)) for t in (1, 2, 3)]
    uppers = call(upper_kernel, ids, (diag_inv,), [whole((4, NB, NB))], (mat,) * 6, (mspec,) * 6)

    def forward(j, w, wspec, own, received):
        return call(
            functools.partial(forward_kernel, j, len(received)), ids, (w, own, lh, ll, *received, *window),
            [wspec, vspec, mspec, mspec, *[vspec] * len(received), *wspecs], (vecb, vec, vec, vecb), (vspec,) * 4,
        )

    y0, w, y_z1, yb = forward(0, rhs, first, yb, moves)
    early = [send(y0, y_move(t)) for t in (1, 2, 3)]
    moves = [send(yb, z_move(1, t)) for t in (2, 3)]
    y1, w, y_z2, yb = forward(1, w, vspec, yb, moves)
    y2_in = send(yb, z_move(2, 3))

    def pick(j):
        d = (j - x + NX) % NX
        return jnp.where(d == 0, same0[0], jnp.where(d == 1, same0[1], jnp.where(d == 2, same0[2], same0[3])))

    p23 = send(pick(3), z_move(2, 3))
    p1 = send(jnp.concatenate([pick(2), pick(3)], axis=1), z_move(1, 3))
    p_same = jnp.concatenate([p23, p1], axis=1)
    p_other = send(p_same, other_core)

    pspec = whole((NB, 3 * HB))
    shape = lambda n: jax.ShapeDtypeStruct((n * NB, cols), BF16)
    y2, y_z3, yb3, xs, x23s, x3s = call(
        turn_kernel, ids, (w, y1, yb, y2_in, lh, ll, *uppers, p_same, p_other, *window, before1, after1, o1, o2, *early),
        [vspec] * 4 + [mspec] * 8 + [pspec] * 2 + wspecs + [ANY] * 7,
        (vecb, vec, vecb, shape(3), shape(2), shape(1)),
        (vspec, vspec, vspec, whole((3 * NB, cols)), whole((2 * NB, cols)), vspec),
        scratch=[pltpu.VMEM((NB, cols), F32)], limit=16,
    )
    to0 = send(xs, z_move(3, 0))
    to1 = send(x23s, z_move(3, 1))
    to2 = send(x3s, z_move(3, 2))
    hold = (top1, bottom1, before2, after2, a1, b1)
    late = call(
        late_kernel, ids, (to0, to1, to2, y1, y2, yb3, *hold),
        [whole((3 * NB, cols)), whole((2 * NB, cols))] + [vspec] * 4 + [ANY] * len(hold),
        shape(3), whole((3 * NB, cols)),
    )
    spread = [send(late, y_move(t)) for t in (1, 2, 3)]
    y_own = jnp.where(z == 0, y_z0, jnp.where(z == 1, y_z1, jnp.where(z == 2, y_z2, y_z3)))
    v0 = jnp.where(owner, y0, early[0] + early[1] + early[2])
    v = jnp.where(owner, late, spread[0] + spread[1] + spread[2])
    v_all = jnp.concatenate([v0, v], axis=0)

    tile = part // 2
    block = pl.BlockSpec((tile, HB), lambda i, ids: (i, 0))
    fixed = whole((tile, HB))
    vall_spec = whole((4 * NB, cols))
    out = jax.ShapeDtypeStruct((rows, cols), F32)

    def product(n, distances, source, buffer, near, far):
        at = pl.BlockSpec(
            (pl.Element(tile), pl.Element(cols)), lambda i, ids: (pl.multiple_of(NB + n * part + i * tile, 128), 0)
        )
        buffers = () if buffer is None else (buffer,)
        alias = {3: 0} if buffers else ({1: 0} if source is not rhs else {})
        return call(
            functools.partial(rows_kernel, distances, bool(buffers)), ids, (source, v_all, *buffers, *near, *far),
            [at, vall_spec] + [ANY] * len(buffers) + [block] * len(near) + [fixed] * len(far),
            out, at, grid=(2,), aliases=alias,
        )

    done = product(0, (0, 1, 3), rhs, None, (own1, o1, after1, a1, before1, b1), (top1, t1, bottom1, u1))
    done = product(1, (0, 1, 3), rhs, done, (own2, o2, after2, a2, before2, b2), ())
    done = call(
        window_kernel, ids, (done, rhs, y_own, v0, v, uppers[0], uppers[1], *window),
        [ANY, first, vspec, vspec, whole((3 * NB, cols)), mspec, mspec, *wspecs],
        out, first, scratch=[pltpu.VMEM((NB, cols), F32)], aliases={1: 0},
    )
    return product(1, (), done, None, (), (top2, t2, bottom2, u2))


def solution(mesh):
    placed = (P("col", "row"), P("col", "row"), P())
    return jax.shard_map(body, mesh=mesh, in_specs=placed, out_specs=P("col", "row"), check_vma=False)
```

```python
import functools

import jax
import jax.numpy as jnp
from jax import lax
from jax.experimental import pallas as pl
from jax.experimental.pallas import tpu as pltpu
from jax.sharding import PartitionSpec as P

NX, NH, NZ, NY = 4, 2, 4, 4
NB = 512
HB = 256
F32, BF16 = jnp.float32, jnp.bfloat16


def pairs(move):
    out = []
    for r in range(NX * NH):
        for c in range(NZ * NY):
            x, h = divmod(r, NH)
            z, y = divmod(c, NY)
            to = move(x, h, z, y)
            if to is not None:
                x2, h2, z2, y2 = to
                out.append((r * NZ * NY + c, ((x2 % NX) * NH + h2 % NH) * NZ * NY + (z2 % NZ) * NY + y2 % NY))
    return out


def send(value, move):
    return lax.ppermute(value, ("row", "col"), pairs(move))


def other_core(x, h, z, y):
    return (x, 1 - h, z, y)


def z_move(src, dst):
    return lambda x, h, z, y: (x, h, dst, y) if (y == 0 and z == src) else None


def y_move(step):
    return lambda x, h, z, y: (x, h, z, step) if y == 0 else None


def dot(a, b):
    return jnp.dot(a, b, preferred_element_type=F32)


def split(a):
    hi = a.astype(BF16)
    return hi, (a - hi.astype(F32)).astype(BF16)


def apply(hi_ref, lo_ref, v):
    vh, vl = split(v)
    return dot(hi_ref[...], vh) + (dot(hi_ref[...], vl) + dot(lo_ref[...], vh))


def lower_mask(d):
    i = lax.broadcasted_iota(jnp.int32, d.shape, 0)
    j = lax.broadcasted_iota(jnp.int32, d.shape, 1)
    return jnp.where(i > j, d, 0.0)


def upper_mask(d):
    i = lax.broadcasted_iota(jnp.int32, d.shape, 0)
    j = lax.broadcasted_iota(jnp.int32, d.shape, 1)
    return jnp.where(i <= j, d, 0.0)


def start_kernel(ids, b_ref, d_ref, y_ref, yb_ref, lh_ref, ll_ref):
    lh_ref[...], ll_ref[...] = split(lower_mask(d_ref[0]))
    w = b_ref[...]
    y = w + apply(lh_ref, ll_ref, w)
    y_ref[...] = y
    yb_ref[...] = y.astype(BF16)


def upper_kernel(ids, d_ref, *out):
    for n, j in enumerate((ids[2], 1, 2)):
        out[2 * n][...], out[2 * n + 1][...] = split(upper_mask(d_ref[j]))


def own_or_received(ids, j, own_ref, received):
    total = received[0][...]
    for piece in received[1:]:
        total = total + piece[...]
    return jnp.where(ids[2] == j, own_ref[...], total)


def columns(j):
    return slice(j * NB, (j + 1) * NB)


def forward_kernel(j, ids, w_ref, own_ref, prior_ref, lh_ref, ll_ref, f_ref, *rest):
    received, (v_ref, w_out, y_ref, yb_ref) = rest[:-4], rest[-4:]
    v = own_or_received(ids, j, own_ref, received)
    v_ref[...] = v
    w = w_ref[...] - dot(f_ref[...], v)
    w_out[...] = w
    y = w + apply(lh_ref, ll_ref, w)
    y_ref[...] = jnp.where(ids[2] == j + 1, y, prior_ref[...])
    yb_ref[...] = y.astype(BF16)


def pick_kernel(ids, f2_ref, f3_ref, after_ref, p23_ref, p1_ref):
    p23_ref[...] = f3_ref[...]
    p1_ref[:, 0:HB] = f2_ref[...]
    p1_ref[:, HB:] = f3_ref[...]


def turn_kernel(
    ids, w_ref, y1_ref, own_ref, y2_in, prior_ref, lh, ll, u3h, u3l, u1h, u1l, u2h, u2l, f_ref, p23, p23_other, p1, p1_other,
    e1, e2, e3, y2_ref, y_ref, yb_ref, x_ref, x23_ref, x3_ref,
):
    h = ids[1]
    y2 = own_or_received(ids, 2, own_ref, (y2_in,))
    y2_ref[...] = y2
    w = w_ref[...] - dot(f_ref[...], y2)
    y3 = w + apply(lh, ll, w)
    y_ref[...] = jnp.where(ids[2] == 3, y3, prior_ref[...])
    yb_ref[...] = y3.astype(BF16)

    def product(same, other, row):
        return dot(same, x_ref[pl.ds(pl.multiple_of(row + h * HB, HB), HB), :]) + dot(
            other, x_ref[pl.ds(pl.multiple_of(row + (1 - h) * HB, HB), HB), :]
        )

    x3 = apply(u3h, u3l, y3).astype(BF16)
    x_ref[2 * NB :, :] = x3
    x23_ref[NB:, :] = x3
    x3_ref[...] = x3
    t = y2.astype(F32) - product(p23[...], p23_other[...], 2 * NB)
    x2 = apply(u2h, u2l, t).astype(BF16)
    x_ref[NB : 2 * NB, :] = x2
    x23_ref[0:NB, :] = x2
    t = y1_ref[...].astype(F32) - product(p1[:, 0:HB], p1_other[:, 0:HB], NB) - product(p1[:, HB:], p1_other[:, HB:], 2 * NB)
    x_ref[0:NB, :] = apply(u1h, u1l, t).astype(BF16)


def late_kernel(ids, to0, to1, to2, y1, y2, y3, *rest):
    late_ref, z = rest[-1], ids[2]
    late_ref[0:NB, :] = jnp.where(z >= 1, y1[...], to0[0:NB, :])
    late_ref[NB : 2 * NB, :] = jnp.where(z >= 2, y2[...], to0[NB : 2 * NB, :] + to1[0:NB, :])
    late_ref[2 * NB :, :] = jnp.where(z >= 3, y3[...], to0[2 * NB :, :] + to1[NB:, :] + to2[...])


def rows_kernel(ids, b_ref, f_ref, v0, e1, e2, e3, late, s1, s2, s3, own_ref, uh_ref, ul_ref, out_ref, v_ref):
    z, owner = ids[2], ids[3] == 0
    window = jnp.logical_and(owner, pl.program_id(0) == 0)

    @pl.when(pl.program_id(0) == 0)
    def _():
        v_ref[0:NB, :] = jnp.where(owner, v0[...], e1[...] + e2[...] + e3[...])
        v_ref[NB:, :] = jnp.where(owner, late[...], s1[...] + s2[...] + s3[...])

    @pl.when(window)
    def _():
        out_ref[...] = own_ref[...]
        for j in range(1, NZ):
            @pl.when(j > z)
            def _():
                out_ref[...] -= dot(f_ref[:, columns(j)], v_ref[columns(j), :])
        out_ref[...] = apply(uh_ref, ul_ref, out_ref[...])

    @pl.when(jnp.logical_not(window))
    def _():
        out_ref[...] = b_ref[...] - dot(f_ref[...], v_ref[...])


def whole(shape):
    return pl.BlockSpec(memory_space=pltpu.VMEM)


def in_hbm(a):
    return pltpu.with_memory_space_constraint(a, pltpu.HBM)


ANY = pl.BlockSpec(memory_space=pl.ANY)


def call(kernel, ids, args, specs, outs, scratch=(), grid=(1,), out_spec=None, limit=12):
    out_specs = jax.tree.map(lambda o: whole(o.shape), outs) if out_spec is None else out_spec
    return pl.pallas_call(
        kernel,
        grid_spec=pltpu.PrefetchScalarGridSpec(
            num_scalar_prefetch=1, grid=grid, in_specs=specs, out_specs=out_specs, scratch_shapes=scratch
        ),
        out_shape=outs,
        cost_estimate=pl.CostEstimate(flops=1, bytes_accessed=1, transcendentals=0),
        compiler_params=pltpu.CompilerParams(vmem_limit_bytes=limit * 1024 * 1024),
    )(ids, *args)


def body(rhs, factors, diag_inv):
    rows, cols = rhs.shape
    r, c = lax.axis_index("row"), lax.axis_index("col")
    ids = jnp.stack([r // NH, r % NH, c // NY, c % NY]).astype(jnp.int32)

    def bf(n, width=cols):
        return jax.ShapeDtypeStruct((n, width), BF16)

    vec, mat = jax.ShapeDtypeStruct((NB, cols), F32), bf(NB, NB)
    vspec, mspec = whole((NB, cols)), whole((NB, NB))
    first = pl.BlockSpec((NB, cols), lambda i, ids: (0, 0))

    window = lax.all_gather(factors[:NB], "row", axis=1, tiled=True)
    gathered = lax.all_gather(factors, "row", axis=1, tiled=True)

    y_z0, yb0, lh, ll = call(
        start_kernel, ids, (in_hbm(rhs), in_hbm(diag_inv)), [first, pl.BlockSpec((1, NB, NB), lambda i, ids: (ids[2], 0, 0))],
        (vec, bf(NB), mat, mat), limit=16,
    )
    hops = [send(yb0, z_move(0, t)) for t in (1, 2, 3)]
    uppers = call(upper_kernel, ids, (in_hbm(diag_inv),), [pl.BlockSpec((4, NB, NB), lambda i, ids: (0, 0, 0))], (mat,) * 6, limit=16)
    wide = lambda j: pl.BlockSpec((NB, NB), lambda i, ids: (0, j))
    half = lambda j: pl.BlockSpec((NB, HB), lambda i, ids: (0, NH * j + ids[1]))

    def forward(j, w, wspec, own, prior, received):
        return call(
            functools.partial(forward_kernel, j), ids, (w, own, prior, lh, ll, in_hbm(window), *received),
            [wspec, vspec, vspec, mspec, mspec, wide(j)] + [vspec] * len(received), (bf(NB), vec, vec, bf(NB)),
        )

    y0, w, y_own, yb1 = forward(0, in_hbm(rhs), first, yb0, y_z0, hops)
    hops = [send(yb1, z_move(1, t)) for t in (2, 3)]
    p23, p1 = call(
        pick_kernel, ids, (in_hbm(window), in_hbm(window), yb1), [half(2), half(3), ANY], (bf(NB, HB), bf(NB, 2 * HB))
    )
    p23 = send(p23, z_move(2, 3))
    p1 = send(p1, z_move(1, 3))
    early = [send(y0, y_move(t)) for t in (1, 2, 3)]
    y1, w, y_own, yb2 = forward(1, w, vspec, yb1, y_own, hops)
    y2_in = send(yb2, z_move(2, 3))
    p23_other, p1_other = send(p23, other_core), send(p1, other_core)
    y2, y_own, yb3, xs, x23s, x3s = call(
        turn_kernel, ids,
        (w, y1, yb2, y2_in, y_own, lh, ll, *uppers, in_hbm(window), p23, p23_other, p1, p1_other, *early),
        [vspec] * 5 + [mspec] * 8 + [wide(2)] + [whole((NB, HB))] * 2 + [mspec] * 2 + [ANY] * 3,
        (bf(NB), vec, bf(NB), bf(3 * NB), bf(2 * NB), bf(NB)),
    )
    to0, to1, to2 = send(xs, z_move(3, 0)), send(x23s, z_move(3, 1)), send(x3s, z_move(3, 2))
    late = call(
        late_kernel, ids, (to0, to1, to2, y1, y2, yb3),
        [whole((3 * NB, cols)), whole((2 * NB, cols))] + [vspec] * 4, bf(3 * NB),
    )
    spread = [send(late, y_move(t)) for t in (1, 2, 3)]
    tile = pl.BlockSpec((NB, cols), lambda i, ids: (i, 0))
    return call(
        rows_kernel, ids, (in_hbm(rhs), in_hbm(gathered), y0, *early, late, *spread, y_own, uppers[0], uppers[1]),
        [tile, pl.BlockSpec((NB, 4 * NB), lambda i, ids: (i, 0))] + [vspec] * 4 + [whole((3 * NB, cols))] * 4
        + [vspec] + [mspec] * 2,
        jax.ShapeDtypeStruct((rows, cols), F32), scratch=[pltpu.VMEM((4 * NB, cols), BF16)],
        grid=(rows // NB,), out_spec=tile, limit=24,
    )


def solution(mesh):
    placed = (P("col", "row"), P("col", "row"), P())
    return jax.shard_map(body, mesh=mesh, in_specs=placed, out_specs=P("col", "row"), check_vma=False)
```

```python
import functools

import jax
import jax.numpy as jnp
from jax import lax
from jax.experimental import pallas as pl
from jax.experimental.pallas import tpu as pltpu
from jax.sharding import PartitionSpec as P

NX, NH, NZ, NY = 4, 2, 4, 4
NB = 512
HB = 256
F32, BF16 = jnp.float32, jnp.bfloat16


def pairs(move):
    out = []
    for r in range(NX * NH):
        for c in range(NZ * NY):
            x, h = divmod(r, NH)
            z, y = divmod(c, NY)
            to = move(x, h, z, y)
            if to is not None:
                x2, h2, z2, y2 = to
                out.append((r * NZ * NY + c, ((x2 % NX) * NH + h2 % NH) * NZ * NY + (z2 % NZ) * NY + y2 % NY))
    return out


def send(value, move):
    return lax.ppermute(value, ("row", "col"), pairs(move))


def x_plus(x, h, z, y):
    return (x + 1, h, z, y)


def x_minus(x, h, z, y):
    return (x - 1, h, z, y)


def x_far(x, h, z, y):
    return (x + 2, h, z, y)


def other_core(x, h, z, y):
    return (x, 1 - h, z, y)


def z_move(src, dst):
    return lambda x, h, z, y: (x, h, dst, y) if (y == 0 and z == src) else None


def y_move(step):
    return lambda x, h, z, y: (x, h, z, step) if y == 0 else None


def dot(a, b):
    return jnp.dot(a, b, preferred_element_type=F32)


def split(a):
    hi = a.astype(BF16)
    return hi, (a - hi.astype(F32)).astype(BF16)


def apply(hi_ref, lo_ref, v):
    vh, vl = split(v)
    return dot(hi_ref[...], vh) + (dot(hi_ref[...], vl) + dot(lo_ref[...], vh))


def lower_mask(d):
    i = lax.broadcasted_iota(jnp.int32, d.shape, 0)
    j = lax.broadcasted_iota(jnp.int32, d.shape, 1)
    return jnp.where(i > j, d, 0.0)


def upper_mask(d):
    i = lax.broadcasted_iota(jnp.int32, d.shape, 0)
    j = lax.broadcasted_iota(jnp.int32, d.shape, 1)
    return jnp.where(i <= j, d, 0.0)


def start_kernel(ids, b_ref, d_ref, y_ref, yb_ref, lh_ref, ll_ref):
    lh_ref[...], ll_ref[...] = split(lower_mask(d_ref[0]))
    w = b_ref[...]
    y = w + apply(lh_ref, ll_ref, w)
    y_ref[...] = y
    yb_ref[...] = y.astype(BF16)


def upper_kernel(ids, d_ref, *out):
    for n, j in enumerate((ids[2], 1, 2)):
        out[2 * n][...], out[2 * n + 1][...] = split(upper_mask(d_ref[j]))


def own_or_received(ids, j, own_ref, received):
    total = received[0][...]
    for piece in received[1:]:
        total = total + piece[...]
    return jnp.where(ids[2] == j, own_ref[...], total)


def block_product(ids, blocks, j, v_ref, acc_ref):
    x, h = ids[0], ids[1]
    for d in range(NX):
        @pl.when(lax.rem(x + d, NX) == j)
        def _():
            same, other = blocks[2 * d], blocks[2 * d + 1]
            acc_ref[...] -= dot(same[...], v_ref[pl.ds(pl.multiple_of(h * HB, HB), HB), :]) + dot(
                other[...], v_ref[pl.ds(pl.multiple_of((1 - h) * HB, HB), HB), :]
            )


def forward_kernel(j, count, ids, w_ref, own_ref, prior_ref, lh_ref, ll_ref, *rest):
    blocks, received, (v_ref, w_out, y_ref, yb_ref) = rest[:8], rest[8 : 8 + count], rest[-4:]
    v_ref[...] = own_or_received(ids, j, own_ref, received)
    w_out[...] = w_ref[...]
    block_product(ids, blocks, j, v_ref, w_out)
    w = w_out[...]
    y = w + apply(lh_ref, ll_ref, w)
    y_ref[...] = jnp.where(ids[2] == j + 1, y, prior_ref[...])
    yb_ref[...] = y.astype(BF16)


def pick_kernel(ids, b0, b1, b2, b3, p23_ref, p1_ref):
    for d, block in enumerate((b0, b1, b2, b3)):
        @pl.when(lax.rem(ids[0] + d, NX) == 2)
        def _():
            p1_ref[:, 0:HB] = block[...]

        @pl.when(lax.rem(ids[0] + d, NX) == 3)
        def _():
            p23_ref[...] = block[...]
            p1_ref[:, HB:] = block[...]


def relay_kernel(ids, p23_ref, p1_ref, after_ref, q23_ref, q1_ref):
    q23_ref[...] = p23_ref[...]
    q1_ref[...] = p1_ref[...]


def turn_kernel(
    ids, w_ref, y1_ref, own_ref, y2_in, prior_ref, lh, ll, u3h, u3l, u1h, u1l, u2h, u2l, p23, p23_other, p1, p1_other, *rest
):
    blocks, (y2_ref, y_ref, yb_ref, x_ref, x23_ref, x3_ref, acc) = rest[:8], rest[-7:]
    h = ids[1]
    y2 = own_or_received(ids, 2, own_ref, (y2_in,))
    y2_ref[...] = y2
    acc[...] = w_ref[...]
    block_product(ids, blocks, 2, y2_ref, acc)
    w = acc[...]
    y3 = w + apply(lh, ll, w)
    y_ref[...] = jnp.where(ids[2] == 3, y3, prior_ref[...])
    yb_ref[...] = y3.astype(BF16)

    def product(same, other, row):
        return dot(same, x_ref[pl.ds(pl.multiple_of(row + h * HB, HB), HB), :]) + dot(
            other, x_ref[pl.ds(pl.multiple_of(row + (1 - h) * HB, HB), HB), :]
        )

    x3 = apply(u3h, u3l, y3).astype(BF16)
    x_ref[2 * NB :, :] = x3
    x23_ref[NB:, :] = x3
    x3_ref[...] = x3
    t = y2.astype(F32) - product(p23[...], p23_other[...], 2 * NB)
    x2 = apply(u2h, u2l, t).astype(BF16)
    x_ref[NB : 2 * NB, :] = x2
    x23_ref[0:NB, :] = x2
    t = y1_ref[...].astype(F32) - product(p1[:, 0:HB], p1_other[:, 0:HB], NB) - product(p1[:, HB:], p1_other[:, HB:], 2 * NB)
    x_ref[0:NB, :] = apply(u1h, u1l, t).astype(BF16)


def late_kernel(ids, to0, to1, to2, y1, y2, y3, *rest):
    late_ref, z = rest[-1], ids[2]
    late_ref[0:NB, :] = jnp.where(z >= 1, y1[...], to0[0:NB, :])
    late_ref[NB : 2 * NB, :] = jnp.where(z >= 2, y2[...], to0[NB : 2 * NB, :] + to1[0:NB, :])
    late_ref[2 * NB :, :] = jnp.where(z >= 3, y3[...], to0[2 * NB :, :] + to1[NB:, :] + to2[...])


def window_kernel(ids, b_ref, v0, e1, e2, e3, late, s1, s2, s3, own_ref, uh_ref, ul_ref, *rest):
    blocks, (out_ref, v_ref, acc) = rest[:8], rest[8:]
    x, h, z, owner = ids[0], ids[1], ids[2], ids[3] == 0
    v_ref[0:NB, :] = jnp.where(owner, v0[...], e1[...] + e2[...] + e3[...])
    v_ref[NB:, :] = jnp.where(owner, late[...], s1[...] + s2[...] + s3[...])
    acc[...] = jnp.where(owner, own_ref[...], b_ref[...])
    for d in range(NX):
        j = lax.rem(x + d, NX)
        for s in range(2):
            part = h if s == 0 else 1 - h

            @pl.when(jnp.logical_or(jnp.logical_not(owner), j > z))
            def _():
                acc[...] -= dot(blocks[2 * d + s][...], v_ref[pl.ds(pl.multiple_of(j * NB + part * HB, HB), HB), :])

    @pl.when(owner)
    def _():
        out_ref[...] = apply(uh_ref, ul_ref, acc[...])

    @pl.when(jnp.logical_not(owner))
    def _():
        out_ref[...] = acc[...]


def rows_kernel(ids, out_in, b_ref, f_ref, v_ref, out_ref):
    out_ref[...] = b_ref[...] - dot(f_ref[...], v_ref[...])


def whole(shape):
    return pl.BlockSpec(memory_space=pltpu.VMEM)


def in_hbm(a):
    return pltpu.with_memory_space_constraint(a, pltpu.HBM)


ANY = pl.BlockSpec(memory_space=pl.ANY)


def call(kernel, ids, args, specs, outs, scratch=(), grid=(1,), out_spec=None, limit=12, aliases={}):
    out_specs = jax.tree.map(lambda o: whole(o.shape), outs) if out_spec is None else out_spec
    return pl.pallas_call(
        kernel,
        grid_spec=pltpu.PrefetchScalarGridSpec(
            num_scalar_prefetch=1, grid=grid, in_specs=specs, out_specs=out_specs, scratch_shapes=scratch
        ),
        out_shape=outs,
        input_output_aliases=aliases,
        cost_estimate=pl.CostEstimate(flops=1, bytes_accessed=1, transcendentals=0),
        compiler_params=pltpu.CompilerParams(vmem_limit_bytes=limit * 1024 * 1024),
    )(ids, *args)


def body(rhs, factors, diag_inv):
    rows, cols = rhs.shape
    r, c = lax.axis_index("row"), lax.axis_index("col")
    ids = jnp.stack([r // NH, r % NH, c // NY, c % NY]).astype(jnp.int32)

    def bf(n, width=cols):
        return jax.ShapeDtypeStruct((n, width), BF16)

    vec, mat = jax.ShapeDtypeStruct((NB, cols), F32), bf(NB, NB)
    vspec, mspec = whole((NB, cols)), whole((NB, NB))
    first = pl.BlockSpec((NB, cols), lambda i, ids: (0, 0))

    own = factors[:NB]
    same = [own, send(own, x_minus), send(own, x_far), send(own, x_plus)]
    gathered = lax.all_gather(factors[NB:], "row", axis=1, tiled=True)
    window = [b for s in same for b in (s, send(s, other_core))]
    wspecs = [whole((NB, HB))] * 8

    y_z0, yb0, lh, ll = call(
        start_kernel, ids, (in_hbm(rhs), in_hbm(diag_inv)), [first, pl.BlockSpec((1, NB, NB), lambda i, ids: (ids[2], 0, 0))],
        (vec, bf(NB), mat, mat), limit=16,
    )
    hops = [send(yb0, z_move(0, t)) for t in (1, 2, 3)]
    uppers = call(upper_kernel, ids, (in_hbm(diag_inv),), [pl.BlockSpec((4, NB, NB), lambda i, ids: (0, 0, 0))], (mat,) * 6, limit=16)
    p23, p1 = call(pick_kernel, ids, same, [whole((NB, HB))] * 4, (bf(NB, HB), bf(NB, 2 * HB)))
    p23 = send(p23, z_move(2, 3))
    p1 = send(p1, z_move(1, 3))

    def forward(j, w, wspec, own, prior, received, after=()):
        return call(
            functools.partial(forward_kernel, j, len(received)), ids, (w, own, prior, lh, ll, *window, *received, *after),
            [wspec, vspec, vspec, mspec, mspec, *wspecs] + [vspec] * len(received) + [ANY] * len(after), (bf(NB), vec, vec, bf(NB)),
        )

    y0, w, y_own, yb1 = forward(0, in_hbm(rhs), first, yb0, y_z0, hops)
    hops = [send(yb1, z_move(1, t)) for t in (2, 3)]
    early = [send(y0, y_move(t)) for t in (1, 2, 3)]
    y1, w, y_own, yb2 = forward(1, w, vspec, yb1, y_own, hops, early)
    y2_in = send(yb2, z_move(2, 3))
    p23, p1 = call(relay_kernel, ids, (p23, p1, yb2), [whole((NB, HB)), mspec, ANY], (bf(NB, HB), bf(NB, 2 * HB)))
    p23_other, p1_other = send(p23, other_core), send(p1, other_core)
    y2, y_own, yb3, xs, x23s, x3s = call(
        turn_kernel, ids,
        (w, y1, yb2, y2_in, y_own, lh, ll, *uppers, p23, p23_other, p1, p1_other, *window),
        [vspec] * 5 + [mspec] * 8 + [whole((NB, HB))] * 2 + [mspec] * 2 + wspecs,
        (bf(NB), vec, bf(NB), bf(3 * NB), bf(2 * NB), bf(NB)), scratch=[pltpu.VMEM((NB, cols), F32)],
    )
    to0, to1, to2 = send(xs, z_move(3, 0)), send(x23s, z_move(3, 1)), send(x3s, z_move(3, 2))
    late = call(
        late_kernel, ids, (to0, to1, to2, y1, y2, yb3),
        [whole((3 * NB, cols)), whole((2 * NB, cols))] + [vspec] * 4, bf(3 * NB),
    )
    spread = [send(late, y_move(t)) for t in (1, 2, 3)]
    out = jax.ShapeDtypeStruct((rows, cols), F32)
    vall = bf(4 * NB)
    done, v = call(
        window_kernel, ids, (in_hbm(rhs), y0, *early, late, *spread, y_own, uppers[0], uppers[1], *window),
        [first] + [vspec] * 4 + [whole((3 * NB, cols))] * 4 + [vspec] + [mspec] * 2 + wspecs,
        (out, vall), out_spec=(first, whole(vall.shape)), scratch=[pltpu.VMEM((NB, cols), F32)],
    )
    tile = (rows - NB) // 4
    at = pl.BlockSpec(
        (pl.Element(tile), pl.Element(cols)), lambda i, ids: (pl.multiple_of(NB + i * tile, 128), 0)
    )
    return call(
        rows_kernel, ids, (done, in_hbm(rhs), in_hbm(gathered), v),
        [ANY, at, pl.BlockSpec((tile, 4 * NB), lambda i, ids: (i, 0)), whole(vall.shape)],
        out, grid=(4,), out_spec=at, limit=32, aliases={1: 0},
    )


def solution(mesh):
    placed = (P("col", "row"), P("col", "row"), P())
    return jax.shard_map(body, mesh=mesh, in_specs=placed, out_specs=P("col", "row"), check_vma=False)
```

```python
import functools

import jax
import jax.numpy as jnp
from jax import lax
from jax.experimental import pallas as pl
from jax.experimental.pallas import tpu as pltpu
from jax.sharding import PartitionSpec as P

NX, NH, NZ, NY = 4, 2, 4, 4
NB = 512
HB = 256
F32, BF16 = jnp.float32, jnp.bfloat16


def pairs(move):
    out = []
    for r in range(NX * NH):
        for c in range(NZ * NY):
            x, h = divmod(r, NH)
            z, y = divmod(c, NY)
            to = move(x, h, z, y)
            if to is not None:
                x2, h2, z2, y2 = to
                out.append((r * NZ * NY + c, ((x2 % NX) * NH + h2 % NH) * NZ * NY + (z2 % NZ) * NY + y2 % NY))
    return out


def send(value, move):
    return lax.ppermute(value, ("row", "col"), pairs(move))


def x_plus(x, h, z, y):
    return (x + 1, h, z, y)


def x_minus(x, h, z, y):
    return (x - 1, h, z, y)


def x_far(x, h, z, y):
    return (x + 2, h, z, y)


def other_core(x, h, z, y):
    return (x, 1 - h, z, y)


def z_move(src, dst):
    return lambda x, h, z, y: (x, h, dst, y) if (y == 0 and z == src) else None


def y_move(step):
    return lambda x, h, z, y: (x, h, z, step) if y == 0 else None


def dot(a, b):
    return jnp.dot(a, b, preferred_element_type=F32)


def split(a):
    hi = a.astype(BF16)
    return hi, (a - hi.astype(F32)).astype(BF16)


def apply(hi_ref, lo_ref, v):
    vh, vl = split(v)
    wide = dot(hi_ref[...], jnp.concatenate([vh, vl], axis=1))
    return wide[:, 0:128] + (wide[:, 128:] + dot(lo_ref[...], vh))


def lower_mask(d):
    i = lax.broadcasted_iota(jnp.int32, d.shape, 0)
    j = lax.broadcasted_iota(jnp.int32, d.shape, 1)
    return jnp.where(i > j, d, 0.0)


def upper_mask(d):
    i = lax.broadcasted_iota(jnp.int32, d.shape, 0)
    j = lax.broadcasted_iota(jnp.int32, d.shape, 1)
    return jnp.where(i <= j, d, 0.0)


def start_kernel(ids, b_ref, d_ref, y_ref, yb_ref, lh_ref, ll_ref):
    lh_ref[...], ll_ref[...] = split(lower_mask(d_ref[0]))
    w = b_ref[...]
    y = w + apply(lh_ref, ll_ref, w)
    y_ref[...] = y
    yb_ref[...] = y.astype(BF16)


def upper_kernel(ids, d_ref, *out):
    for n, j in enumerate((ids[2], 1, 2)):
        out[2 * n][...], out[2 * n + 1][...] = split(upper_mask(d_ref[j]))


def combine_kernel(ids, own_ref, r1, r2, r3, v_ref):
    v_ref[...] = own_or_received(ids, 0, own_ref, (r1, r2, r3))


def own_or_received(ids, j, own_ref, received):
    if not received:
        return own_ref[...]
    total = received[0][...]
    for piece in received[1:]:
        total = total + piece[...]
    return jnp.where(ids[2] == j, own_ref[...], total)


def block_product(ids, blocks, j, v_ref, acc_ref):
    x, h = ids[0], ids[1]
    for d in range(NX):
        @pl.when(lax.rem(x + d, NX) == j)
        def _():
            same, other = blocks[2 * d], blocks[2 * d + 1]
            acc_ref[...] -= dot(same[...], v_ref[pl.ds(pl.multiple_of(h * HB, HB), HB), :]) + dot(
                other[...], v_ref[pl.ds(pl.multiple_of((1 - h) * HB, HB), HB), :]
            )


def forward_kernel(j, count, ids, w_ref, own_ref, prior_ref, lh_ref, ll_ref, *rest):
    blocks, received, (v_ref, w_out, y_ref, yb_ref) = rest[:8], rest[8 : 8 + count], rest[-4:]
    v_ref[...] = own_or_received(ids, j, own_ref, received)
    w_out[...] = w_ref[...]
    block_product(ids, blocks, j, v_ref, w_out)
    w = w_out[...]
    y = w + apply(lh_ref, ll_ref, w)
    y_ref[...] = jnp.where(ids[2] == j + 1, y, prior_ref[...])
    yb_ref[...] = y.astype(BF16)


def pick_kernel(ids, b0, b1, b2, b3, p23_ref, p1_ref):
    for d, block in enumerate((b0, b1, b2, b3)):
        @pl.when(lax.rem(ids[0] + d, NX) == 2)
        def _():
            p1_ref[:, 0:HB] = block[...]

        @pl.when(lax.rem(ids[0] + d, NX) == 3)
        def _():
            p23_ref[...] = block[...]
            p1_ref[:, HB:] = block[...]


def relay_kernel(ids, p23_ref, p1_ref, after_ref, q23_ref, q1_ref):
    q23_ref[...] = p23_ref[...]
    q1_ref[...] = p1_ref[...]


def turn_kernel(
    ids, w_ref, y1_ref, own_ref, y2_in, prior_ref, lh, ll, u3h, u3l, u1h, u1l, u2h, u2l, p23, p23_other, p1, p1_other, *rest
):
    blocks, (y2_ref, y_ref, yb_ref, x_ref, x23_ref, x3_ref, acc) = rest[:8], rest[-7:]
    h = ids[1]
    y2 = own_or_received(ids, 2, own_ref, (y2_in,))
    y2_ref[...] = y2
    acc[...] = w_ref[...]
    block_product(ids, blocks, 2, y2_ref, acc)
    w = acc[...]
    y3 = w + apply(lh, ll, w)
    y_ref[...] = jnp.where(ids[2] == 3, y3, prior_ref[...])
    yb_ref[...] = y3.astype(BF16)

    def product(same, other, row):
        return dot(same, x_ref[pl.ds(pl.multiple_of(row + h * HB, HB), HB), :]) + dot(
            other, x_ref[pl.ds(pl.multiple_of(row + (1 - h) * HB, HB), HB), :]
        )

    x3 = apply(u3h, u3l, y3).astype(BF16)
    x_ref[2 * NB :, :] = x3
    x23_ref[NB:, :] = x3
    x3_ref[...] = x3
    t = y2.astype(F32) - product(p23[...], p23_other[...], 2 * NB)
    x2 = apply(u2h, u2l, t).astype(BF16)
    x_ref[NB : 2 * NB, :] = x2
    x23_ref[0:NB, :] = x2
    t = y1_ref[...].astype(F32) - product(p1[:, 0:HB], p1_other[:, 0:HB], NB) - product(p1[:, HB:], p1_other[:, HB:], 2 * NB)
    x_ref[0:NB, :] = apply(u1h, u1l, t).astype(BF16)


def late_kernel(ids, to0, to1, to2, y1, y2, y3, *rest):
    late_ref, z = rest[-1], ids[2]
    late_ref[0:NB, :] = jnp.where(z >= 1, y1[...], to0[0:NB, :])
    late_ref[NB : 2 * NB, :] = jnp.where(z >= 2, y2[...], to0[NB : 2 * NB, :] + to1[0:NB, :])
    late_ref[2 * NB :, :] = jnp.where(z >= 3, y3[...], to0[2 * NB :, :] + to1[NB:, :] + to2[...])


def unknowns_kernel(ids, v0, e1, e2, e3, late, s1, s2, s3, v_ref, mine_ref, theirs_ref):
    h, owner = ids[1], ids[3] == 0
    v_ref[0:NB, :] = jnp.where(owner, v0[...], e1[...] + e2[...] + e3[...])
    v_ref[NB:, :] = jnp.where(owner, late[...], s1[...] + s2[...] + s3[...])
    for j in range(4):
        rows = slice(j * HB, (j + 1) * HB)
        mine_ref[rows, :] = v_ref[pl.ds(pl.multiple_of(j * NB + h * HB, HB), HB), :]
        theirs_ref[rows, :] = v_ref[pl.ds(pl.multiple_of(j * NB + (1 - h) * HB, HB), HB), :]


def window_kernel(ids, b_ref, v_ref, own_ref, uh_ref, ul_ref, *rest):
    blocks, (out_ref, acc) = rest[:8], rest[8:]
    x, h, z, owner = ids[0], ids[1], ids[2], ids[3] == 0
    acc[...] = jnp.where(owner, own_ref[...], b_ref[...])
    for d in range(NX):
        j = lax.rem(x + d, NX)
        for s in range(2):
            part = h if s == 0 else 1 - h

            @pl.when(jnp.logical_or(jnp.logical_not(owner), j > z))
            def _():
                acc[...] -= dot(blocks[2 * d + s][...], v_ref[pl.ds(pl.multiple_of(j * NB + part * HB, HB), HB), :])

    @pl.when(owner)
    def _():
        out_ref[...] = apply(uh_ref, ul_ref, acc[...])

    @pl.when(jnp.logical_not(owner))
    def _():
        out_ref[...] = acc[...]


def rows_kernel(ids, out_in, b_ref, mine_ref, other_ref, *rest):
    blocks, (out_ref, part_ref, v_ref) = rest[:4], rest[4:]

    @pl.when(pl.program_id(0) == 0)
    def _():
        v_ref[:, 0:128] = mine_ref[...]
        v_ref[:, 128:] = other_ref[...]

    total = None
    for d in range(NX):
        j = lax.rem(ids[0] + d, NX)
        term = dot(blocks[d][...], v_ref[pl.ds(pl.multiple_of(j * HB, HB), HB), :])
        total = term if total is None else total + term
    out_ref[...] = b_ref[...] - total[:, 0:128]
    part_ref[...] = total[:, 128:].astype(BF16)


def add_kernel(ids, a_ref, part_ref, out_ref):
    out_ref[...] = a_ref[...] - part_ref[...].astype(F32)


def whole(shape):
    return pl.BlockSpec(memory_space=pltpu.VMEM)


def in_hbm(a):
    return pltpu.with_memory_space_constraint(a, pltpu.HBM)


ANY = pl.BlockSpec(memory_space=pl.ANY)


def call(kernel, ids, args, specs, outs, scratch=(), grid=(1,), out_spec=None, limit=12, aliases={}):
    out_specs = jax.tree.map(lambda o: whole(o.shape), outs) if out_spec is None else out_spec
    return pl.pallas_call(
        kernel,
        grid_spec=pltpu.PrefetchScalarGridSpec(
            num_scalar_prefetch=1, grid=grid, in_specs=specs, out_specs=out_specs, scratch_shapes=scratch
        ),
        out_shape=outs,
        input_output_aliases=aliases,
        cost_estimate=pl.CostEstimate(flops=1, bytes_accessed=1, transcendentals=0),
        compiler_params=pltpu.CompilerParams(vmem_limit_bytes=limit * 1024 * 1024),
    )(ids, *args)


def body(rhs, factors, diag_inv):
    rows, cols = rhs.shape
    r, c = lax.axis_index("row"), lax.axis_index("col")
    ids = jnp.stack([r // NH, r % NH, c // NY, c % NY]).astype(jnp.int32)

    def bf(n, width=cols):
        return jax.ShapeDtypeStruct((n, width), BF16)

    vec, mat = jax.ShapeDtypeStruct((NB, cols), F32), bf(NB, NB)
    vspec, mspec = whole((NB, cols)), whole((NB, NB))
    first = pl.BlockSpec((NB, cols), lambda i, ids: (0, 0))

    own = factors[:NB]
    same = [own, send(own, x_minus), send(own, x_far), send(own, x_plus)]
    half = (rows - NB) // 2
    own_t, own_b = factors[NB : NB + half], factors[NB + half :]
    before_t, after_b = send(own_t, x_plus), send(own_b, x_minus)
    before_b, after_t = send(own_b, x_plus), send(own_t, x_minus)
    far_t, far_b = send(before_t, x_plus), send(after_b, x_minus)
    window = [b for s in same for b in (s, send(s, other_core))]
    wspecs = [whole((NB, HB))] * 8

    y_z0, yb0, lh, ll = call(
        start_kernel, ids, (in_hbm(rhs), in_hbm(diag_inv)), [first, pl.BlockSpec((1, NB, NB), lambda i, ids: (ids[2], 0, 0))],
        (vec, bf(NB), mat, mat), limit=16,
    )
    hops = [send(yb0, z_move(0, t)) for t in (1, 2, 3)]
    uppers = call(upper_kernel, ids, (in_hbm(diag_inv),), [pl.BlockSpec((4, NB, NB), lambda i, ids: (0, 0, 0))], (mat,) * 6, limit=16)
    p23, p1 = call(pick_kernel, ids, same, [whole((NB, HB))] * 4, (bf(NB, HB), bf(NB, 2 * HB)))
    p23 = send(p23, z_move(2, 3))
    p1 = send(p1, z_move(1, 3))

    def forward(j, w, wspec, own, prior, received, after=()):
        return call(
            functools.partial(forward_kernel, j, len(received)), ids, (w, own, prior, lh, ll, *window, *received, *after),
            [wspec, vspec, vspec, mspec, mspec, *wspecs] + [vspec] * len(received) + [ANY] * len(after), (bf(NB), vec, vec, bf(NB)),
        )

    y0 = call(combine_kernel, ids, (yb0, *hops), [vspec] * 4, bf(NB))
    early = [send(y0, y_move(t)) for t in (1, 2, 3)]
    _, w, y_own, yb1 = forward(0, in_hbm(rhs), first, y0, y_z0, ())
    hops = [send(yb1, z_move(1, t)) for t in (2, 3)]
    y1, w, y_own, yb2 = forward(1, w, vspec, yb1, y_own, hops, (*early, before_t, after_b))
    y2_in = send(yb2, z_move(2, 3))
    p23, p1 = call(relay_kernel, ids, (p23, p1, yb2), [whole((NB, HB)), mspec, ANY], (bf(NB, HB), bf(NB, 2 * HB)))
    p23_other, p1_other = send(p23, other_core), send(p1, other_core)
    y2, y_own, yb3, xs, x23s, x3s = call(
        turn_kernel, ids,
        (w, y1, yb2, y2_in, y_own, lh, ll, *uppers, p23, p23_other, p1, p1_other, *window),
        [vspec] * 5 + [mspec] * 8 + [whole((NB, HB))] * 2 + [mspec] * 2 + wspecs,
        (bf(NB), vec, bf(NB), bf(3 * NB), bf(2 * NB), bf(NB)), scratch=[pltpu.VMEM((NB, cols), F32)],
    )
    to0, to1, to2 = send(xs, z_move(3, 0)), send(x23s, z_move(3, 1)), send(x3s, z_move(3, 2))
    late = call(
        late_kernel, ids, (to0, to1, to2, y1, y2, yb3, before_b, after_t),
        [whole((3 * NB, cols)), whole((2 * NB, cols))] + [vspec] * 4 + [ANY] * 2, bf(3 * NB),
    )
    spread = [send(late, y_move(t)) for t in (1, 2, 3)]
    out = jax.ShapeDtypeStruct((rows, cols), F32)
    v, mine, theirs = call(
        unknowns_kernel, ids, (y0, *early, late, *spread), [vspec] * 4 + [whole((3 * NB, cols))] * 4,
        (bf(4 * NB), bf(4 * HB), bf(4 * HB)),
    )
    other = send(theirs, other_core)
    done = call(
        window_kernel, ids, (in_hbm(rhs), v, y_own, uppers[0], uppers[1], *window),
        [first, whole((4 * NB, cols)), vspec, mspec, mspec, *wspecs], out, out_spec=first, scratch=[pltpu.VMEM((NB, cols), F32)],
    )
    tile = half // 2
    near = pl.BlockSpec((tile, HB), lambda i, ids: (i, 0))
    narrow = pl.BlockSpec((tile, cols), lambda i, ids: (i, 0))

    def at(n):
        return pl.BlockSpec(
            (pl.Element(tile), pl.Element(cols)), lambda i, ids: (pl.multiple_of(NB + n * half + i * tile, 128), 0)
        )

    parts = []
    for n, blocks in enumerate(((own_t, after_t, far_t, before_t), (own_b, after_b, far_b, before_b))):
        done, part = call(
            rows_kernel, ids, (done, in_hbm(rhs), mine, other, *blocks),
            [ANY, at(n), whole(mine.shape), whole(mine.shape)] + [near] * 4,
            (out, bf(half)), grid=(2,), out_spec=(at(n), narrow), scratch=[pltpu.VMEM((4 * HB, 2 * cols), BF16)],
            limit=24, aliases={1: 0},
        )
        parts.append(send(part, other_core))
    for n, part in enumerate(parts):
        done = call(add_kernel, ids, (done, part), [at(n), narrow], out, grid=(2,), out_spec=at(n), aliases={1: 0})
    return done


def solution(mesh):
    placed = (P("col", "row"), P("col", "row"), P())
    return jax.shard_map(body, mesh=mesh, in_specs=placed, out_specs=P("col", "row"), check_vma=False)
```

```python
import functools

import jax
import jax.numpy as jnp
from jax import lax
from jax.experimental import pallas as pl
from jax.experimental.pallas import tpu as pltpu
from jax.sharding import PartitionSpec as P

NX, NH, NZ, NY = 4, 2, 4, 4
NB = 512
HB = 256
F32, BF16 = jnp.float32, jnp.bfloat16


def pairs(move):
    out = []
    for r in range(NX * NH):
        for c in range(NZ * NY):
            x, h = divmod(r, NH)
            z, y = divmod(c, NY)
            to = move(x, h, z, y)
            if to is not None:
                x2, h2, z2, y2 = to
                out.append((r * NZ * NY + c, ((x2 % NX) * NH + h2 % NH) * NZ * NY + (z2 % NZ) * NY + y2 % NY))
    return out


def send(value, move):
    return lax.ppermute(value, ("row", "col"), pairs(move))


def x_plus(x, h, z, y):
    return (x + 1, h, z, y)


def x_minus(x, h, z, y):
    return (x - 1, h, z, y)


def x_far(x, h, z, y):
    return (x + 2, h, z, y)


def other_core(x, h, z, y):
    return (x, 1 - h, z, y)


def z_move(src, dst):
    return lambda x, h, z, y: (x, h, dst, y) if (y == 0 and z == src) else None


def y_move(step):
    return lambda x, h, z, y: (x, h, z, step) if y == 0 else None


def dot(a, b):
    return jnp.dot(a, b, preferred_element_type=F32)


def split(a):
    hi = a.astype(BF16)
    return hi, (a - hi.astype(F32)).astype(BF16)


def apply(hi_ref, lo_ref, v):
    vh, vl = split(v)
    wide = dot(hi_ref[...], jnp.concatenate([vh, vl], axis=1))
    return wide[:, 0:128] + (wide[:, 128:] + dot(lo_ref[...], vh))


def lower_mask(d):
    i = lax.broadcasted_iota(jnp.int32, d.shape, 0)
    j = lax.broadcasted_iota(jnp.int32, d.shape, 1)
    return jnp.where(i > j, d, 0.0)


def upper_mask(d):
    i = lax.broadcasted_iota(jnp.int32, d.shape, 0)
    j = lax.broadcasted_iota(jnp.int32, d.shape, 1)
    return jnp.where(i <= j, d, 0.0)


def start_kernel(ids, b_ref, d_ref, after_ref, y_ref, yb_ref, lh_ref, ll_ref):
    lh_ref[...], ll_ref[...] = split(lower_mask(d_ref[0]))
    w = b_ref[...]
    y = w + apply(lh_ref, ll_ref, w)
    y_ref[...] = y
    yb_ref[...] = y.astype(BF16)


def upper_kernel(ids, d_ref, *out):
    for n, j in enumerate((ids[2], 1, 2)):
        out[2 * n][...], out[2 * n + 1][...] = split(upper_mask(d_ref[j]))


def combine_kernel(ids, own_ref, r1, r2, r3, v_ref):
    v_ref[...] = own_or_received(ids, 0, own_ref, (r1, r2, r3))


def own_or_received(ids, j, own_ref, received):
    if not received:
        return own_ref[...]
    total = received[0][...]
    for piece in received[1:]:
        total = total + piece[...]
    return jnp.where(ids[2] == j, own_ref[...], total)


def block_product(ids, blocks, j, v_ref, acc_ref):
    x, h = ids[0], ids[1]
    for d in range(NX):
        @pl.when(lax.rem(x + d, NX) == j)
        def _():
            same, other = blocks[2 * d], blocks[2 * d + 1]
            acc_ref[...] -= dot(same[...], v_ref[pl.ds(pl.multiple_of(h * HB, HB), HB), :]) + dot(
                other[...], v_ref[pl.ds(pl.multiple_of((1 - h) * HB, HB), HB), :]
            )


def forward_kernel(j, count, ids, w_ref, own_ref, prior_ref, lh_ref, ll_ref, *rest):
    blocks, received, (v_ref, w_out, y_ref, yb_ref) = rest[:8], rest[8 : 8 + count], rest[-4:]
    v_ref[...] = own_or_received(ids, j, own_ref, received)
    w_out[...] = w_ref[...]
    block_product(ids, blocks, j, v_ref, w_out)
    w = w_out[...]
    y = w + apply(lh_ref, ll_ref, w)
    y_ref[...] = jnp.where(ids[2] == j + 1, y, prior_ref[...])
    yb_ref[...] = y.astype(BF16)


def pick_kernel(ids, b0, b1, b2, b3, p23_ref, p1_ref):
    for d, block in enumerate((b0, b1, b2, b3)):
        @pl.when(lax.rem(ids[0] + d, NX) == 2)
        def _():
            p1_ref[:, 0:HB] = block[...]

        @pl.when(lax.rem(ids[0] + d, NX) == 3)
        def _():
            p23_ref[...] = block[...]
            p1_ref[:, HB:] = block[...]


def relay_kernel(ids, p23_ref, p1_ref, after_ref, q23_ref, q1_ref):
    q23_ref[...] = p23_ref[...]
    q1_ref[...] = p1_ref[...]


def turn_kernel(
    ids, w_ref, y1_ref, own_ref, y2_in, prior_ref, lh, ll, u3h, u3l, u1h, u1l, u2h, u2l, p23, p23_other, p1, p1_other, *rest
):
    blocks, (y2_ref, y_ref, yb_ref, x_ref, x23_ref, x3_ref, acc) = rest[:8], rest[-7:]
    h = ids[1]
    y2 = own_or_received(ids, 2, own_ref, (y2_in,))
    y2_ref[...] = y2
    acc[...] = w_ref[...]
    block_product(ids, blocks, 2, y2_ref, acc)
    w = acc[...]
    y3 = w + apply(lh, ll, w)
    y_ref[...] = jnp.where(ids[2] == 3, y3, prior_ref[...])
    yb_ref[...] = y3.astype(BF16)

    def product(same, other, row):
        return dot(same, x_ref[pl.ds(pl.multiple_of(row + h * HB, HB), HB), :]) + dot(
            other, x_ref[pl.ds(pl.multiple_of(row + (1 - h) * HB, HB), HB), :]
        )

    x3 = apply(u3h, u3l, y3).astype(BF16)
    x_ref[2 * NB :, :] = x3
    x23_ref[NB:, :] = x3
    x3_ref[...] = x3
    t = y2.astype(F32) - product(p23[...], p23_other[...], 2 * NB)
    x2 = apply(u2h, u2l, t).astype(BF16)
    x_ref[NB : 2 * NB, :] = x2
    x23_ref[0:NB, :] = x2
    t = y1_ref[...].astype(F32) - product(p1[:, 0:HB], p1_other[:, 0:HB], NB) - product(p1[:, HB:], p1_other[:, HB:], 2 * NB)
    x_ref[0:NB, :] = apply(u1h, u1l, t).astype(BF16)


def late_kernel(ids, to0, to1, to2, y0, y1, y2, y3, *rest):
    late_ref, z = rest[-1], ids[2]
    late_ref[0:NB, :] = y0[...]
    late_ref[NB : 2 * NB, :] = jnp.where(z >= 1, y1[...], to0[0:NB, :])
    late_ref[2 * NB : 3 * NB, :] = jnp.where(z >= 2, y2[...], to0[NB : 2 * NB, :] + to1[0:NB, :])
    late_ref[3 * NB :, :] = jnp.where(z >= 3, y3[...], to0[2 * NB :, :] + to1[NB:, :] + to2[...])


def unknowns_kernel(ids, late, s1, s2, s3, v_ref, mine_ref, theirs_ref):
    h, owner = ids[1], ids[3] == 0
    v_ref[...] = jnp.where(owner, late[...], s1[...] + s2[...] + s3[...])
    for j in range(4):
        rows = slice(j * HB, (j + 1) * HB)
        mine_ref[rows, :] = v_ref[pl.ds(pl.multiple_of(j * NB + h * HB, HB), HB), :]
        theirs_ref[rows, :] = v_ref[pl.ds(pl.multiple_of(j * NB + (1 - h) * HB, HB), HB), :]


def window_kernel(ids, b_ref, v_ref, own_ref, uh_ref, ul_ref, *rest):
    blocks, (out_ref, acc) = rest[:8], rest[8:]
    x, h, z, owner = ids[0], ids[1], ids[2], ids[3] == 0
    acc[...] = jnp.where(owner, own_ref[...], b_ref[...])
    for d in range(NX):
        j = lax.rem(x + d, NX)
        for s in range(2):
            part = h if s == 0 else 1 - h

            @pl.when(jnp.logical_or(jnp.logical_not(owner), j > z))
            def _():
                acc[...] -= dot(blocks[2 * d + s][...], v_ref[pl.ds(pl.multiple_of(j * NB + part * HB, HB), HB), :])

    @pl.when(owner)
    def _():
        out_ref[...] = apply(uh_ref, ul_ref, acc[...])

    @pl.when(jnp.logical_not(owner))
    def _():
        out_ref[...] = acc[...]


def rows_kernel(tiles, ids, mine_ref, other_ref, *rest):
    blocks, (own_ref, part_ref, v_ref) = rest[:4], rest[4:]
    v_ref[:, 0:128] = mine_ref[...]
    v_ref[:, 128:] = other_ref[...]
    tile = own_ref.shape[0] // tiles
    for t in range(tiles):
        rows = slice(t * tile, (t + 1) * tile)
        total = None
        for d in range(NX):
            j = lax.rem(ids[0] + d, NX)
            term = dot(blocks[d][rows, :], v_ref[pl.ds(pl.multiple_of(j * HB, HB), HB), :])
            total = term if total is None else total + term
        own_ref[rows, :] = total[:, 0:128]
        part_ref[rows, :] = total[:, 128:].astype(BF16)


def add_kernel(ids, out_in, b_ref, own_t, part_t, own_b, part_b, out_ref):
    i, n = pl.program_id(0), b_ref.shape[0]
    half = own_t.shape[0] // n
    for top, own, part in ((True, own_t, part_t), (False, own_b, part_b)):
        @pl.when((i < half) == top)
        def _():
            rows = pl.ds(pl.multiple_of((i if top else i - half) * n, n), n)
            out_ref[...] = b_ref[...] - own[rows, :] - part[rows, :].astype(F32)


def whole(shape):
    return pl.BlockSpec(memory_space=pltpu.VMEM)


def in_hbm(a):
    return pltpu.with_memory_space_constraint(a, pltpu.HBM)


ANY = pl.BlockSpec(memory_space=pl.ANY)


def call(kernel, ids, args, specs, outs, scratch=(), grid=(1,), out_spec=None, limit=12, aliases={}):
    out_specs = jax.tree.map(lambda o: whole(o.shape), outs) if out_spec is None else out_spec
    return pl.pallas_call(
        kernel,
        grid_spec=pltpu.PrefetchScalarGridSpec(
            num_scalar_prefetch=1, grid=grid, in_specs=specs, out_specs=out_specs, scratch_shapes=scratch
        ),
        out_shape=outs,
        input_output_aliases=aliases,
        cost_estimate=pl.CostEstimate(flops=1, bytes_accessed=1, transcendentals=0),
        compiler_params=pltpu.CompilerParams(vmem_limit_bytes=limit * 1024 * 1024),
    )(ids, *args)


def body(rhs, factors, diag_inv):
    rows, cols = rhs.shape
    r, c = lax.axis_index("row"), lax.axis_index("col")
    ids = jnp.stack([r // NH, r % NH, c // NY, c % NY]).astype(jnp.int32)

    def bf(n, width=cols):
        return jax.ShapeDtypeStruct((n, width), BF16)

    vec, mat = jax.ShapeDtypeStruct((NB, cols), F32), bf(NB, NB)
    vspec, mspec = whole((NB, cols)), whole((NB, NB))
    first = pl.BlockSpec((NB, cols), lambda i, ids: (0, 0))

    own = factors[:NB]
    same = [own, send(own, x_minus), send(own, x_far), send(own, x_plus)]
    half = (rows - NB) // 2
    own_t, own_b = factors[NB : NB + half], factors[NB + half :]
    before_t, after_b = send(own_t, x_plus), send(own_b, x_minus)
    before_b, after_t = send(own_b, x_plus), send(own_t, x_minus)
    far_t, far_b = send(before_t, x_plus), send(after_b, x_minus)
    window = [b for s in same for b in (s, send(s, other_core))]
    wspecs = [whole((NB, HB))] * 8

    y_z0, yb0, lh, ll = call(
        start_kernel, ids, (in_hbm(rhs), in_hbm(diag_inv), own), [first, pl.BlockSpec((1, NB, NB), lambda i, ids: (ids[2], 0, 0)), ANY],
        (vec, bf(NB), mat, mat), limit=16,
    )
    hops = [send(yb0, z_move(0, t)) for t in (1, 2, 3)]
    uppers = call(upper_kernel, ids, (in_hbm(diag_inv),), [pl.BlockSpec((4, NB, NB), lambda i, ids: (0, 0, 0))], (mat,) * 6, limit=16)
    p23, p1 = call(pick_kernel, ids, same, [whole((NB, HB))] * 4, (bf(NB, HB), bf(NB, 2 * HB)))
    p23 = send(p23, z_move(2, 3))
    p1 = send(p1, z_move(1, 3))

    def forward(j, w, wspec, own, prior, received, after=()):
        return call(
            functools.partial(forward_kernel, j, len(received)), ids, (w, own, prior, lh, ll, *window, *received, *after),
            [wspec, vspec, vspec, mspec, mspec, *wspecs] + [vspec] * len(received) + [ANY] * len(after), (bf(NB), vec, vec, bf(NB)),
        )

    y0 = call(combine_kernel, ids, (yb0, *hops), [vspec] * 4, bf(NB))
    y0, w, y_own, yb1 = forward(0, in_hbm(rhs), first, y0, y_z0, ())
    hops = [send(yb1, z_move(1, t)) for t in (2, 3)]
    y1, w, y_own, yb2 = forward(1, w, vspec, yb1, y_own, hops)
    y2_in = send(yb2, z_move(2, 3))
    p23, p1 = call(relay_kernel, ids, (p23, p1, yb2), [whole((NB, HB)), mspec, ANY], (bf(NB, HB), bf(NB, 2 * HB)))
    p23_other, p1_other = send(p23, other_core), send(p1, other_core)
    y2, y_own, yb3, xs, x23s, x3s = call(
        turn_kernel, ids,
        (w, y1, yb2, y2_in, y_own, lh, ll, *uppers, p23, p23_other, p1, p1_other, *window, before_t, after_b),
        [vspec] * 5 + [mspec] * 8 + [whole((NB, HB))] * 2 + [mspec] * 2 + wspecs + [ANY] * 2,
        (bf(NB), vec, bf(NB), bf(3 * NB), bf(2 * NB), bf(NB)), scratch=[pltpu.VMEM((NB, cols), F32)],
    )
    to0, to1, to2 = send(xs, z_move(3, 0)), send(x23s, z_move(3, 1)), send(x3s, z_move(3, 2))
    late = call(
        late_kernel, ids, (to0, to1, to2, y0, y1, y2, yb3, before_b, after_t),
        [whole((3 * NB, cols)), whole((2 * NB, cols))] + [vspec] * 5 + [ANY] * 2, bf(4 * NB),
    )
    spread = [send(late, y_move(t)) for t in (1, 2, 3)]
    out = jax.ShapeDtypeStruct((rows, cols), F32)
    v, mine, theirs = call(
        unknowns_kernel, ids, (late, *spread), [whole((4 * NB, cols))] * 4,
        (bf(4 * NB), bf(4 * HB), bf(4 * HB)),
    )
    other = send(theirs, other_core)
    done = call(
        window_kernel, ids, (in_hbm(rhs), v, y_own, uppers[0], uppers[1], *window),
        [first, whole((4 * NB, cols)), vspec, mspec, mspec, *wspecs], out, out_spec=first, scratch=[pltpu.VMEM((NB, cols), F32)],
    )
    sums, parts = [], []
    for blocks in ((own_t, after_t, far_t, before_t), (own_b, after_b, far_b, before_b)):
        total, part = call(
            functools.partial(rows_kernel, 2), ids, (mine, other, *blocks),
            [vspec] * 2 + [mspec] * 4, (jax.ShapeDtypeStruct((half, cols), F32), bf(half)),
            scratch=[pltpu.VMEM((4 * HB, 2 * cols), BF16)], limit=24,
        )
        sums.append(total)
        parts.append(send(part, other_core))
    tile = half // 2
    at = pl.BlockSpec((pl.Element(tile), pl.Element(cols)), lambda i, ids: (pl.multiple_of(NB + i * tile, 128), 0))
    return call(
        add_kernel, ids, (done, in_hbm(rhs), sums[0], parts[0], sums[1], parts[1]),
        [ANY, at] + [vspec] * 4, out, grid=(4,), out_spec=at, aliases={1: 0},
    )


def solution(mesh):
    placed = (P("col", "row"), P("col", "row"), P())
    return jax.shard_map(body, mesh=mesh, in_specs=placed, out_specs=P("col", "row"), check_vma=False)
```

```python
import functools

import jax
import jax.numpy as jnp
from jax import lax
from jax.experimental import pallas as pl
from jax.experimental.pallas import tpu as pltpu
from jax.sharding import PartitionSpec as P

NX, NH, NZ, NY = 4, 2, 4, 4
NB = 512
HB = 256
F32, BF16 = jnp.float32, jnp.bfloat16


def pairs(move):
    out = []
    for r in range(NX * NH):
        for c in range(NZ * NY):
            x, h = divmod(r, NH)
            z, y = divmod(c, NY)
            to = move(x, h, z, y)
            if to is not None:
                x2, h2, z2, y2 = to
                out.append((r * NZ * NY + c, ((x2 % NX) * NH + h2 % NH) * NZ * NY + (z2 % NZ) * NY + y2 % NY))
    return out


def send(value, move):
    return lax.ppermute(value, ("row", "col"), pairs(move))


def x_plus(x, h, z, y):
    return (x + 1, h, z, y)


def x_minus(x, h, z, y):
    return (x - 1, h, z, y)


def x_far(x, h, z, y):
    return (x + 2, h, z, y)


def other_core(x, h, z, y):
    return (x, 1 - h, z, y)


def z_move(src, dst):
    return lambda x, h, z, y: (x, h, dst, y) if (y == 0 and z == src) else None


def y_move(step):
    return lambda x, h, z, y: (x, h, z, step) if y == 0 else None


def dot(a, b):
    return jnp.dot(a, b, preferred_element_type=F32)


def split(a):
    hi = a.astype(BF16)
    return hi, (a - hi.astype(F32)).astype(BF16)


def apply(hi_ref, lo_ref, v):
    vh, vl = split(v)
    wide = dot(hi_ref[...], jnp.concatenate([vh, vl], axis=1))
    return wide[:, 0:128] + (wide[:, 128:] + dot(lo_ref[...], vh))


def lower_mask(d):
    i = lax.broadcasted_iota(jnp.int32, d.shape, 0)
    j = lax.broadcasted_iota(jnp.int32, d.shape, 1)
    return jnp.where(i > j, d, 0.0)


def upper_mask(d):
    i = lax.broadcasted_iota(jnp.int32, d.shape, 0)
    j = lax.broadcasted_iota(jnp.int32, d.shape, 1)
    return jnp.where(i <= j, d, 0.0)


def start_kernel(ids, b_ref, d_ref, after_ref, y_ref, yb_ref, lh_ref, ll_ref):
    lh_ref[...], ll_ref[...] = split(lower_mask(d_ref[0]))
    w = b_ref[...]
    y = w + apply(lh_ref, ll_ref, w)
    y_ref[...] = y
    yb_ref[...] = y.astype(BF16)


def upper_kernel(ids, d_ref, *out):
    for n, j in enumerate((ids[2], 1, 2)):
        out[2 * n][...], out[2 * n + 1][...] = split(upper_mask(d_ref[j]))


def combine_kernel(ids, own_ref, r1, r2, r3, v_ref):
    v_ref[...] = own_or_received(ids, 0, own_ref, (r1, r2, r3))


def own_or_received(ids, j, own_ref, received):
    if not received:
        return own_ref[...]
    total = received[0][...]
    for piece in received[1:]:
        total = total + piece[...]
    return jnp.where(ids[2] == j, own_ref[...], total)


def block_product(ids, blocks, j, v_ref, acc_ref):
    x, h = ids[0], ids[1]
    for d in range(NX):
        @pl.when(lax.rem(x + d, NX) == j)
        def _():
            same, other = blocks[2 * d], blocks[2 * d + 1]
            acc_ref[...] -= dot(same[...], v_ref[pl.ds(pl.multiple_of(h * HB, HB), HB), :]) + dot(
                other[...], v_ref[pl.ds(pl.multiple_of((1 - h) * HB, HB), HB), :]
            )


def forward_kernel(j, count, ids, w_ref, own_ref, prior_ref, lh_ref, ll_ref, *rest):
    blocks, received, (v_ref, w_out, y_ref, yb_ref) = rest[:8], rest[8 : 8 + count], rest[-4:]
    v_ref[...] = own_or_received(ids, j, own_ref, received)
    w_out[...] = w_ref[...]
    block_product(ids, blocks, j, v_ref, w_out)
    w = w_out[...]
    y = w + apply(lh_ref, ll_ref, w)
    y_ref[...] = jnp.where(ids[2] == j + 1, y, prior_ref[...])
    if j == 0:
        yb_ref[...] = y.astype(BF16)
    else:
        yb_ref[0:NB, :] = v_ref[...]
        yb_ref[NB:, :] = y.astype(BF16)


def pick_kernel(ids, b0, b1, b2, b3, p23_ref, p1_ref):
    for d, block in enumerate((b0, b1, b2, b3)):
        @pl.when(lax.rem(ids[0] + d, NX) == 2)
        def _():
            p1_ref[:, 0:HB] = block[...]

        @pl.when(lax.rem(ids[0] + d, NX) == 3)
        def _():
            p23_ref[...] = block[...]
            p1_ref[:, HB:] = block[...]


def relay_kernel(ids, p23_ref, p1_ref, after_ref, q23_ref, q1_ref):
    q23_ref[...] = p23_ref[...]
    q1_ref[...] = p1_ref[...]


def turn_kernel(
    ids, w_ref, y12_ref, y12_in, prior_ref, lh, ll, u3h, u3l, u1h, u1l, u2h, u2l, p23, p23_other, p1, p1_other, *rest
):
    blocks, (y1_ref, y2_ref, y_ref, yb_ref, x_ref, x23_ref, x3_ref, acc) = rest[:8], rest[-8:]
    h = ids[1]
    last = ids[2] == 3
    y1_ref[...] = jnp.where(last, y12_in[0:NB, :], y12_ref[0:NB, :])
    y2 = jnp.where(last, y12_in[NB:, :], y12_ref[NB:, :])
    y2_ref[...] = y2
    acc[...] = w_ref[...]
    block_product(ids, blocks, 1, y1_ref, acc)
    block_product(ids, blocks, 2, y2_ref, acc)
    w = acc[...]
    y3 = w + apply(lh, ll, w)
    y_ref[...] = jnp.where(ids[2] == 3, y3, prior_ref[...])
    yb_ref[...] = y3.astype(BF16)

    def product(same, other, row):
        return dot(same, x_ref[pl.ds(pl.multiple_of(row + h * HB, HB), HB), :]) + dot(
            other, x_ref[pl.ds(pl.multiple_of(row + (1 - h) * HB, HB), HB), :]
        )

    x3 = apply(u3h, u3l, y3).astype(BF16)
    x_ref[2 * NB :, :] = x3
    x23_ref[NB:, :] = x3
    x3_ref[...] = x3
    t = y2.astype(F32) - product(p23[...], p23_other[...], 2 * NB)
    x2 = apply(u2h, u2l, t).astype(BF16)
    x_ref[NB : 2 * NB, :] = x2
    x23_ref[0:NB, :] = x2
    t = y1_ref[...].astype(F32) - product(p1[:, 0:HB], p1_other[:, 0:HB], NB) - product(p1[:, HB:], p1_other[:, HB:], 2 * NB)
    x_ref[0:NB, :] = apply(u1h, u1l, t).astype(BF16)


def late_kernel(ids, to0, to1, to2, y0, y1, y2, y3, *rest):
    late_ref, z = rest[-1], ids[2]
    late_ref[0:NB, :] = y0[...]
    late_ref[NB : 2 * NB, :] = jnp.where(z >= 1, y1[...], to0[0:NB, :])
    late_ref[2 * NB : 3 * NB, :] = jnp.where(z >= 2, y2[...], to0[NB : 2 * NB, :] + to1[0:NB, :])
    late_ref[3 * NB :, :] = jnp.where(z >= 3, y3[...], to0[2 * NB :, :] + to1[NB:, :] + to2[...])


def unknowns_kernel(ids, late, s1, s2, s3, v_ref, mine_ref, theirs_ref):
    h, owner = ids[1], ids[3] == 0
    v_ref[...] = jnp.where(owner, late[...], s1[...] + s2[...] + s3[...])
    for j in range(4):
        rows = slice(j * HB, (j + 1) * HB)
        mine_ref[rows, :] = v_ref[pl.ds(pl.multiple_of(j * NB + h * HB, HB), HB), :]
        theirs_ref[rows, :] = v_ref[pl.ds(pl.multiple_of(j * NB + (1 - h) * HB, HB), HB), :]


def window_kernel(ids, b_ref, v_ref, own_ref, uh_ref, ul_ref, *rest):
    blocks, (out_ref, acc) = rest[:8], rest[8:]
    x, h, z, owner = ids[0], ids[1], ids[2], ids[3] == 0
    acc[...] = jnp.where(owner, own_ref[...], b_ref[...])
    for d in range(NX):
        j = lax.rem(x + d, NX)
        for s in range(2):
            part = h if s == 0 else 1 - h

            @pl.when(jnp.logical_or(jnp.logical_not(owner), j > z))
            def _():
                acc[...] -= dot(blocks[2 * d + s][...], v_ref[pl.ds(pl.multiple_of(j * NB + part * HB, HB), HB), :])

    @pl.when(owner)
    def _():
        out_ref[...] = apply(uh_ref, ul_ref, acc[...])

    @pl.when(jnp.logical_not(owner))
    def _():
        out_ref[...] = acc[...]


def rows_kernel(tiles, ids, mine_ref, other_ref, *rest):
    blocks, (own_ref, part_ref, v_ref) = rest[:4], rest[4:]
    v_ref[:, 0:128] = mine_ref[...]
    v_ref[:, 128:] = other_ref[...]
    tile = own_ref.shape[0] // tiles
    for t in range(tiles):
        rows = slice(t * tile, (t + 1) * tile)
        total = None
        for d in range(NX):
            j = lax.rem(ids[0] + d, NX)
            term = dot(blocks[d][rows, :], v_ref[pl.ds(pl.multiple_of(j * HB, HB), HB), :])
            total = term if total is None else total + term
        own_ref[rows, :] = total[:, 0:128]
        part_ref[rows, :] = total[:, 128:].astype(BF16)


def add_kernel(ids, out_in, b_ref, own_t, part_t, own_b, part_b, out_ref):
    i, n = pl.program_id(0), b_ref.shape[0]
    half = own_t.shape[0] // n
    for top, own, part in ((True, own_t, part_t), (False, own_b, part_b)):
        @pl.when((i < half) == top)
        def _():
            rows = pl.ds(pl.multiple_of((i if top else i - half) * n, n), n)
            out_ref[...] = b_ref[...] - own[rows, :] - part[rows, :].astype(F32)


def whole(shape):
    return pl.BlockSpec(memory_space=pltpu.VMEM)


def in_hbm(a):
    return pltpu.with_memory_space_constraint(a, pltpu.HBM)


ANY = pl.BlockSpec(memory_space=pl.ANY)


def call(kernel, ids, args, specs, outs, scratch=(), grid=(1,), out_spec=None, limit=12, aliases={}):
    out_specs = jax.tree.map(lambda o: whole(o.shape), outs) if out_spec is None else out_spec
    return pl.pallas_call(
        kernel,
        grid_spec=pltpu.PrefetchScalarGridSpec(
            num_scalar_prefetch=1, grid=grid, in_specs=specs, out_specs=out_specs, scratch_shapes=scratch
        ),
        out_shape=outs,
        input_output_aliases=aliases,
        cost_estimate=pl.CostEstimate(flops=1, bytes_accessed=1, transcendentals=0),
        compiler_params=pltpu.CompilerParams(vmem_limit_bytes=limit * 1024 * 1024),
    )(ids, *args)


def body(rhs, factors, diag_inv):
    rows, cols = rhs.shape
    r, c = lax.axis_index("row"), lax.axis_index("col")
    ids = jnp.stack([r // NH, r % NH, c // NY, c % NY]).astype(jnp.int32)

    def bf(n, width=cols):
        return jax.ShapeDtypeStruct((n, width), BF16)

    vec, mat = jax.ShapeDtypeStruct((NB, cols), F32), bf(NB, NB)
    vspec, mspec = whole((NB, cols)), whole((NB, NB))
    first = pl.BlockSpec((NB, cols), lambda i, ids: (0, 0))

    own = factors[:NB]
    same = [own, send(own, x_minus), send(own, x_far), send(own, x_plus)]
    half = (rows - NB) // 2
    own_t, own_b = factors[NB : NB + half], factors[NB + half :]
    before_t, after_b = send(own_t, x_plus), send(own_b, x_minus)
    before_b, after_t = send(own_b, x_plus), send(own_t, x_minus)
    far_t, far_b = send(before_t, x_plus), send(after_b, x_minus)
    window = [b for s in same for b in (s, send(s, other_core))]
    wspecs = [whole((NB, HB))] * 8

    y_z0, yb0, lh, ll = call(
        start_kernel, ids, (in_hbm(rhs), in_hbm(diag_inv), own), [first, pl.BlockSpec((1, NB, NB), lambda i, ids: (ids[2], 0, 0)), ANY],
        (vec, bf(NB), mat, mat), limit=16,
    )
    hops = [send(yb0, z_move(0, t)) for t in (1, 2, 3)]
    uppers = call(upper_kernel, ids, (in_hbm(diag_inv),), [pl.BlockSpec((4, NB, NB), lambda i, ids: (0, 0, 0))], (mat,) * 6, limit=16)
    p23, p1 = call(pick_kernel, ids, same, [whole((NB, HB))] * 4, (bf(NB, HB), bf(NB, 2 * HB)))
    p23 = send(p23, z_move(2, 3))
    p1 = send(p1, z_move(1, 3))

    def forward(j, w, wspec, own, prior, received, after=()):
        return call(
            functools.partial(forward_kernel, j, len(received)), ids, (w, own, prior, lh, ll, *window, *received, *after),
            [wspec, vspec, vspec, mspec, mspec, *wspecs] + [vspec] * len(received) + [ANY] * len(after), (bf(NB), vec, vec, bf(NB if j == 0 else 2 * NB)),
        )

    y0 = call(combine_kernel, ids, (yb0, *hops), [vspec] * 4, bf(NB))
    _, w0, y_own, yb1 = forward(0, in_hbm(rhs), first, y0, y_z0, (), uppers)
    hops = [send(yb1, z_move(1, 2))]
    _, _, y_own, y12 = forward(1, w0, vspec, yb1, y_own, hops)
    y12_in = send(y12, z_move(2, 3))
    p23, p1 = call(relay_kernel, ids, (p23, p1, y12), [whole((NB, HB)), mspec, ANY], (bf(NB, HB), bf(NB, 2 * HB)))
    p23_other, p1_other = send(p23, other_core), send(p1, other_core)
    y1, y2, y_own, yb3, xs, x23s, x3s = call(
        turn_kernel, ids,
        (w0, y12, y12_in, y_own, lh, ll, *uppers, p23, p23_other, p1, p1_other, *window, before_t, after_b),
        [vspec] * 4 + [mspec] * 8 + [whole((NB, HB))] * 2 + [mspec] * 2 + wspecs + [ANY] * 2,
        (bf(NB), bf(NB), vec, bf(NB), bf(3 * NB), bf(2 * NB), bf(NB)), scratch=[pltpu.VMEM((NB, cols), F32)],
    )
    to0, to1, to2 = send(xs, z_move(3, 0)), send(x23s, z_move(3, 1)), send(x3s, z_move(3, 2))
    late = call(
        late_kernel, ids, (to0, to1, to2, y0, y1, y2, yb3, before_b, after_t),
        [whole((3 * NB, cols)), whole((2 * NB, cols))] + [vspec] * 5 + [ANY] * 2, bf(4 * NB),
    )
    spread = [send(late, y_move(t)) for t in (1, 2, 3)]
    out = jax.ShapeDtypeStruct((rows, cols), F32)
    v, mine, theirs = call(
        unknowns_kernel, ids, (late, *spread), [whole((4 * NB, cols))] * 4,
        (bf(4 * NB), bf(4 * HB), bf(4 * HB)),
    )
    other = send(theirs, other_core)
    done = call(
        window_kernel, ids, (in_hbm(rhs), v, y_own, uppers[0], uppers[1], *window),
        [first, whole((4 * NB, cols)), vspec, mspec, mspec, *wspecs], out, out_spec=first, scratch=[pltpu.VMEM((NB, cols), F32)],
    )
    sums, parts = [], []
    for blocks in ((own_t, after_t, far_t, before_t), (own_b, after_b, far_b, before_b)):
        total, part = call(
            functools.partial(rows_kernel, 2), ids, (mine, other, *blocks),
            [vspec] * 2 + [mspec] * 4, (jax.ShapeDtypeStruct((half, cols), F32), bf(half)),
            scratch=[pltpu.VMEM((4 * HB, 2 * cols), BF16)], limit=24,
        )
        sums.append(total)
        parts.append(send(part, other_core))
    tile = half // 2
    at = pl.BlockSpec((pl.Element(tile), pl.Element(cols)), lambda i, ids: (pl.multiple_of(NB + i * tile, 128), 0))
    return call(
        add_kernel, ids, (done, in_hbm(rhs), sums[0], parts[0], sums[1], parts[1]),
        [ANY, at] + [vspec] * 4, out, grid=(4,), out_spec=at, aliases={1: 0},
    )


def solution(mesh):
    placed = (P("col", "row"), P("col", "row"), P())
    return jax.shard_map(body, mesh=mesh, in_specs=placed, out_specs=P("col", "row"), check_vma=False)
```

```python
import functools

import jax
import jax.numpy as jnp
from jax import lax
from jax.experimental import pallas as pl
from jax.experimental.pallas import tpu as pltpu
from jax.sharding import PartitionSpec as P

NX, NH, NZ, NY = 4, 2, 4, 4
NB = 512
HB = 256
F32, BF16 = jnp.float32, jnp.bfloat16


def pairs(move):
    out = []
    for r in range(NX * NH):
        for c in range(NZ * NY):
            x, h = divmod(r, NH)
            z, y = divmod(c, NY)
            to = move(x, h, z, y)
            if to is not None:
                x2, h2, z2, y2 = to
                out.append((r * NZ * NY + c, ((x2 % NX) * NH + h2 % NH) * NZ * NY + (z2 % NZ) * NY + y2 % NY))
    return out


def send(value, move):
    return lax.ppermute(value, ("row", "col"), pairs(move))


def x_plus(x, h, z, y):
    return (x + 1, h, z, y)


def x_minus(x, h, z, y):
    return (x - 1, h, z, y)


def x_far(x, h, z, y):
    return (x + 2, h, z, y)


def other_core(x, h, z, y):
    return (x, 1 - h, z, y)


def z_move(src, dst):
    return lambda x, h, z, y: (x, h, dst, y) if (y == 0 and z == src) else None


def y_move(step):
    return lambda x, h, z, y: (x, h, z, step) if y == 0 else None


def dot(a, b):
    return jnp.dot(a, b, preferred_element_type=F32)


def split(a):
    hi = a.astype(BF16)
    return hi, (a - hi.astype(F32)).astype(BF16)


def apply(hi_ref, lo_ref, v):
    vh, vl = split(v)
    wide = dot(hi_ref[...], jnp.concatenate([vh, vl], axis=1))
    return wide[:, 0:128] + (wide[:, 128:] + dot(lo_ref[...], vh))


def lower_mask(d):
    i = lax.broadcasted_iota(jnp.int32, d.shape, 0)
    j = lax.broadcasted_iota(jnp.int32, d.shape, 1)
    return jnp.where(i > j, d, 0.0)


def upper_mask(d):
    i = lax.broadcasted_iota(jnp.int32, d.shape, 0)
    j = lax.broadcasted_iota(jnp.int32, d.shape, 1)
    return jnp.where(i <= j, d, 0.0)


def start_kernel(ids, b_ref, d_ref, after_ref, y_ref, yb_ref, lh_ref, ll_ref, *uppers):
    lh_ref[...], ll_ref[...] = split(lower_mask(d_ref[ids[2]]))
    w = b_ref[...]
    y = w + apply(lh_ref, ll_ref, w)
    y_ref[...] = y
    yb_ref[...] = y.astype(BF16)
    for n, j in enumerate((ids[2], 1, 2)):
        uppers[2 * n][...], uppers[2 * n + 1][...] = split(upper_mask(d_ref[j]))


def combine_kernel(ids, own_ref, r1, r2, r3, v_ref):
    v_ref[...] = own_or_received(ids, 0, own_ref, (r1, r2, r3))


def own_or_received(ids, j, own_ref, received):
    if not received:
        return own_ref[...]
    total = received[0][...]
    for piece in received[1:]:
        total = total + piece[...]
    return jnp.where(ids[2] == j, own_ref[...], total)


def window_blocks(blocks, d):
    return blocks[d], (blocks[4] if d == 0 else blocks[5].at[(d - 1) * NB : d * NB, :])


def block_product(ids, blocks, j, v_ref, acc_ref):
    x, h = ids[0], ids[1]
    for d in range(NX):
        @pl.when(lax.rem(x + d, NX) == j)
        def _():
            same, other = window_blocks(blocks, d)
            acc_ref[...] -= dot(same[...], v_ref[pl.ds(pl.multiple_of(h * HB, HB), HB), :]) + dot(
                other[...], v_ref[pl.ds(pl.multiple_of((1 - h) * HB, HB), HB), :]
            )


def forward_kernel(j, count, ids, w_ref, own_ref, prior_ref, lh_ref, ll_ref, *rest):
    blocks, received, (v_ref, w_out, y_ref, yb_ref) = rest[:6], rest[6 : 6 + count], rest[-4:]
    v_ref[...] = own_or_received(ids, j, own_ref, received)
    w_out[...] = w_ref[...]
    block_product(ids, blocks, j, v_ref, w_out)
    w = w_out[...]
    y = w + apply(lh_ref, ll_ref, w)
    y_ref[...] = jnp.where(ids[2] == j + 1, y, prior_ref[...])
    if j == 0:
        yb_ref[...] = y.astype(BF16)
    else:
        yb_ref[0:NB, :] = v_ref[...]
        yb_ref[NB:, :] = y.astype(BF16)


def pick_kernel(ids, b0, b1, b2, b3, p23_ref, p1_ref, all_ref):
    for d, block in enumerate((b1, b2, b3)):
        all_ref[d * NB : (d + 1) * NB, :] = block[...]
    for d, block in enumerate((b0, b1, b2, b3)):
        @pl.when(lax.rem(ids[0] + d, NX) == 2)
        def _():
            p1_ref[:, 0:HB] = block[...]

        @pl.when(lax.rem(ids[0] + d, NX) == 3)
        def _():
            p23_ref[...] = block[...]
            p1_ref[:, HB:] = block[...]


def relay_kernel(ids, p23_ref, p1_ref, after_ref, q23_ref, q1_ref):
    q23_ref[...] = p23_ref[...]
    q1_ref[...] = p1_ref[...]


def turn_kernel(
    ids, w_ref, y12_ref, y12_in, prior_ref, lh, ll, u3h, u3l, u1h, u1l, u2h, u2l, p23, p23_other, p1, p1_other, *rest
):
    blocks, (y1_ref, y2_ref, y_ref, yb_ref, x_ref, x23_ref, x3_ref, acc) = rest[:6], rest[-8:]
    h = ids[1]
    last = ids[2] == 3
    y1_ref[...] = jnp.where(last, y12_in[0:NB, :], y12_ref[0:NB, :])
    y2 = jnp.where(last, y12_in[NB:, :], y12_ref[NB:, :])
    y2_ref[...] = y2
    acc[...] = w_ref[...]
    block_product(ids, blocks, 1, y1_ref, acc)
    block_product(ids, blocks, 2, y2_ref, acc)
    w = acc[...]
    y3 = w + apply(lh, ll, w)
    y_ref[...] = jnp.where(ids[2] == 3, y3, prior_ref[...])
    yb_ref[...] = y3.astype(BF16)

    def product(same, other, row):
        return dot(same, x_ref[pl.ds(pl.multiple_of(row + h * HB, HB), HB), :]) + dot(
            other, x_ref[pl.ds(pl.multiple_of(row + (1 - h) * HB, HB), HB), :]
        )

    x3 = apply(u3h, u3l, y3).astype(BF16)
    x_ref[2 * NB :, :] = x3
    x23_ref[NB:, :] = x3
    x3_ref[...] = x3
    t = y2.astype(F32) - product(p23[...], p23_other[...], 2 * NB)
    x2 = apply(u2h, u2l, t).astype(BF16)
    x_ref[NB : 2 * NB, :] = x2
    x23_ref[0:NB, :] = x2
    t = y1_ref[...].astype(F32) - product(p1[:, 0:HB], p1_other[:, 0:HB], NB) - product(p1[:, HB:], p1_other[:, HB:], 2 * NB)
    x_ref[0:NB, :] = apply(u1h, u1l, t).astype(BF16)


def hold_kernel(ids, top, bottom, after_ref, top_out, bottom_out):
    top_out[...] = top[...]
    bottom_out[...] = bottom[...]


def late_kernel(ids, to0, to1, to2, y0, y1, y2, y3, *rest):
    late_ref, z = rest[-1], ids[2]
    late_ref[0:NB, :] = y0[...]
    late_ref[NB : 2 * NB, :] = jnp.where(z >= 1, y1[...], to0[0:NB, :])
    late_ref[2 * NB : 3 * NB, :] = jnp.where(z >= 2, y2[...], to0[NB : 2 * NB, :] + to1[0:NB, :])
    late_ref[3 * NB :, :] = jnp.where(z >= 3, y3[...], to0[2 * NB :, :] + to1[NB:, :] + to2[...])


def unknowns_kernel(ids, late, s1, s2, s3, v_ref, mine_ref, theirs_ref):
    h, owner = ids[1], ids[3] == 0
    v_ref[...] = jnp.where(owner, late[...], s1[...] + s2[...] + s3[...])
    for j in range(4):
        rows = slice(j * HB, (j + 1) * HB)
        mine_ref[rows, :] = v_ref[pl.ds(pl.multiple_of(j * NB + h * HB, HB), HB), :]
        theirs_ref[rows, :] = v_ref[pl.ds(pl.multiple_of(j * NB + (1 - h) * HB, HB), HB), :]


def window_kernel(ids, b_ref, v_ref, own_ref, uh_ref, ul_ref, *rest):
    blocks, (out_ref, acc) = rest[:6], rest[6:]
    x, h, z, owner = ids[0], ids[1], ids[2], ids[3] == 0
    acc[...] = jnp.where(owner, own_ref[...], b_ref[...])
    for d in range(NX):
        j = lax.rem(x + d, NX)
        for s in range(2):
            part = h if s == 0 else 1 - h

            @pl.when(jnp.logical_or(jnp.logical_not(owner), j > z))
            def _():
                block = window_blocks(blocks, d)[s]
                acc[...] -= dot(block[...], v_ref[pl.ds(pl.multiple_of(j * NB + part * HB, HB), HB), :])

    @pl.when(owner)
    def _():
        out_ref[...] = apply(uh_ref, ul_ref, acc[...])

    @pl.when(jnp.logical_not(owner))
    def _():
        out_ref[...] = acc[...]


def rows_kernel(tiles, ids, mine_ref, other_ref, *rest):
    blocks, (own_ref, part_ref, v_ref) = rest[:4], rest[4:]
    v_ref[:, 0:128] = mine_ref[...]
    v_ref[:, 128:] = other_ref[...]
    tile = own_ref.shape[0] // tiles
    for t in range(tiles):
        rows = slice(t * tile, (t + 1) * tile)
        total = None
        for d in range(NX):
            j = lax.rem(ids[0] + d, NX)
            term = dot(blocks[d][rows, :], v_ref[pl.ds(pl.multiple_of(j * HB, HB), HB), :])
            total = term if total is None else total + term
        own_ref[rows, :] = total[:, 0:128]
        part_ref[rows, :] = total[:, 128:].astype(BF16)


def add_kernel(ids, out_in, b_ref, own_t, part_t, own_b, part_b, out_ref):
    i, n = pl.program_id(0), out_ref.shape[0]
    half = own_t.shape[0] // n
    for top, own, part in ((True, own_t, part_t), (False, own_b, part_b)):
        @pl.when((i < half) == top)
        def _():
            rows = pl.ds(pl.multiple_of((i if top else i - half) * n, n), n)
            base = b_ref[pl.ds(pl.multiple_of(NB + i * n, 128), n), :]
            out_ref[...] = base - own[rows, :] - part[rows, :].astype(F32)


def whole(shape):
    return pl.BlockSpec(memory_space=pltpu.VMEM)


def in_hbm(a):
    return pltpu.with_memory_space_constraint(a, pltpu.HBM)


ANY = pl.BlockSpec(memory_space=pl.ANY)


def call(kernel, ids, args, specs, outs, scratch=(), grid=(1,), out_spec=None, limit=12, aliases={}):
    out_specs = jax.tree.map(lambda o: whole(o.shape), outs) if out_spec is None else out_spec
    return pl.pallas_call(
        kernel,
        grid_spec=pltpu.PrefetchScalarGridSpec(
            num_scalar_prefetch=1, grid=grid, in_specs=specs, out_specs=out_specs, scratch_shapes=scratch
        ),
        out_shape=outs,
        input_output_aliases=aliases,
        cost_estimate=pl.CostEstimate(flops=1, bytes_accessed=1, transcendentals=0),
        compiler_params=pltpu.CompilerParams(vmem_limit_bytes=limit * 1024 * 1024),
    )(ids, *args)


def body(rhs, factors, diag_inv):
    rows, cols = rhs.shape
    r, c = lax.axis_index("row"), lax.axis_index("col")
    ids = jnp.stack([r // NH, r % NH, c // NY, c % NY]).astype(jnp.int32)

    def bf(n, width=cols):
        return jax.ShapeDtypeStruct((n, width), BF16)

    vec, mat = jax.ShapeDtypeStruct((NB, cols), F32), bf(NB, NB)
    vspec, mspec = whole((NB, cols)), whole((NB, NB))
    first = pl.BlockSpec((NB, cols), lambda i, ids: (0, 0))

    own = factors[:NB]
    same = [own, send(own, x_minus), send(own, x_far), send(own, x_plus)]
    half = (rows - NB) // 2
    own_t, own_b = factors[NB : NB + half], factors[NB + half :]
    before_t, after_b = send(own_t, x_plus), send(own_b, x_minus)
    far_t, far_b = send(before_t, x_plus), send(after_b, x_minus)
    own_other = send(own, other_core)
    wspecs = [whole((NB, HB))] * 6

    y_z0, yb0, lh, ll, *uppers = call(
        start_kernel, ids, (in_hbm(rhs), in_hbm(diag_inv), own), [first, pl.BlockSpec((4, NB, NB), lambda i, ids: (0, 0, 0)), ANY],
        (vec, bf(NB), mat, mat) + (mat,) * 6, limit=16,
    )
    hops = [send(yb0, z_move(0, t)) for t in (1, 2, 3)]
    p23, p1, received = call(
        pick_kernel, ids, same, [whole((NB, HB))] * 4, (bf(NB, HB), bf(NB, 2 * HB), bf(3 * NB, HB))
    )
    window = [*same, own_other, send(received, other_core)]
    p23 = send(p23, z_move(2, 3))
    p1 = send(p1, z_move(1, 3))

    def forward(j, w, wspec, own, prior, received, after=()):
        return call(
            functools.partial(forward_kernel, j, len(received)), ids, (w, own, prior, lh, ll, *window, *received, *after),
            [wspec, vspec, vspec, mspec, mspec, *wspecs] + [vspec] * len(received) + [ANY] * len(after), (bf(NB), vec, vec, bf(NB if j == 0 else 2 * NB)),
        )

    y0 = call(combine_kernel, ids, (yb0, *hops), [vspec] * 4, bf(NB))
    _, w0, y_own, yb1 = forward(0, in_hbm(rhs), first, y0, y_z0, ())
    hops = [send(yb1, z_move(1, 2))]
    _, _, y_own, y12 = forward(1, w0, vspec, yb1, y_own, hops)
    y12_in = send(y12, z_move(2, 3))
    top, bottom = call(hold_kernel, ids, (own_t, own_b, y12_in), [whole((half, HB))] * 2 + [ANY], (bf(half, HB),) * 2)
    before_b, after_t = send(bottom, x_plus), send(top, x_minus)
    p23, p1 = call(relay_kernel, ids, (p23, p1, y12), [whole((NB, HB)), mspec, ANY], (bf(NB, HB), bf(NB, 2 * HB)))
    p23_other, p1_other = send(p23, other_core), send(p1, other_core)
    y1, y2, y_own, yb3, xs, x23s, x3s = call(
        turn_kernel, ids,
        (w0, y12, y12_in, y_own, lh, ll, *uppers, p23, p23_other, p1, p1_other, *window, before_t, after_b),
        [vspec] * 4 + [mspec] * 8 + [whole((NB, HB))] * 2 + [mspec] * 2 + wspecs + [ANY] * 2,
        (bf(NB), bf(NB), vec, bf(NB), bf(3 * NB), bf(2 * NB), bf(NB)), scratch=[pltpu.VMEM((NB, cols), F32)],
    )
    to0, to1, to2 = send(xs, z_move(3, 0)), send(x23s, z_move(3, 1)), send(x3s, z_move(3, 2))
    late = call(
        late_kernel, ids, (to0, to1, to2, y0, y1, y2, yb3, before_b, after_t),
        [whole((3 * NB, cols)), whole((2 * NB, cols))] + [vspec] * 5 + [ANY] * 2, bf(4 * NB),
    )
    spread = [send(late, y_move(t)) for t in (1, 2, 3)]
    out = jax.ShapeDtypeStruct((rows, cols), F32)
    v, mine, theirs = call(
        unknowns_kernel, ids, (late, *spread), [whole((4 * NB, cols))] * 4,
        (bf(4 * NB), bf(4 * HB), bf(4 * HB)),
    )
    other = send(theirs, other_core)
    done = call(
        window_kernel, ids, (in_hbm(rhs), v, y_own, uppers[0], uppers[1], *window),
        [first, whole((4 * NB, cols)), vspec, mspec, mspec, *wspecs], out, out_spec=first, scratch=[pltpu.VMEM((NB, cols), F32)],
    )
    sums, parts = [], []
    for blocks in ((own_t, after_t, far_t, before_t), (own_b, after_b, far_b, before_b)):
        total, part = call(
            functools.partial(rows_kernel, 2), ids, (mine, other, *blocks),
            [vspec] * 2 + [mspec] * 4, (jax.ShapeDtypeStruct((half, cols), F32), bf(half)),
            scratch=[pltpu.VMEM((4 * HB, 2 * cols), BF16)], limit=24,
        )
        sums.append(total)
        parts.append(send(part, other_core))
    tile = half // 2
    at = pl.BlockSpec((pl.Element(tile), pl.Element(cols)), lambda i, ids: (pl.multiple_of(NB + i * tile, 128), 0))
    return call(
        add_kernel, ids, (done, rhs, sums[0], parts[0], sums[1], parts[1]),
        [ANY] + [vspec] * 5, out, grid=(4,), out_spec=at, aliases={1: 0},
    )


def solution(mesh):
    placed = (P("col", "row"), P("col", "row"), P())
    return jax.shard_map(body, mesh=mesh, in_specs=placed, out_specs=P("col", "row"), check_vma=False)
```

```python
import functools

import jax
import jax.numpy as jnp
from jax import lax
from jax.experimental import pallas as pl
from jax.experimental.pallas import tpu as pltpu
from jax.sharding import PartitionSpec as P

NX, NH, NZ, NY = 4, 2, 4, 4
NB = 512
HB = 256
F32, BF16 = jnp.float32, jnp.bfloat16


def pairs(move):
    out = []
    for r in range(NX * NH):
        for c in range(NZ * NY):
            x, h = divmod(r, NH)
            z, y = divmod(c, NY)
            to = move(x, h, z, y)
            if to is not None:
                x2, h2, z2, y2 = to
                out.append((r * NZ * NY + c, ((x2 % NX) * NH + h2 % NH) * NZ * NY + (z2 % NZ) * NY + y2 % NY))
    return out


def send(value, move):
    return lax.ppermute(value, ("row", "col"), pairs(move))


def x_plus(x, h, z, y):
    return (x + 1, h, z, y)


def x_minus(x, h, z, y):
    return (x - 1, h, z, y)


def x_far(x, h, z, y):
    return (x + 2, h, z, y)


def other_core(x, h, z, y):
    return (x, 1 - h, z, y)


def z_move(src, dst):
    return lambda x, h, z, y: (x, h, dst, y) if (y == 0 and z == src) else None


def y_move(step):
    return lambda x, h, z, y: (x, h, z, step) if y == 0 else None


def dot(a, b):
    return jnp.dot(a, b, preferred_element_type=F32)


def split(a):
    hi = a.astype(BF16)
    return hi, (a - hi.astype(F32)).astype(BF16)


def apply(hi_ref, lo_ref, v):
    vh, vl = split(v)
    wide = dot(hi_ref[...], jnp.concatenate([vh, vl], axis=1))
    return wide[:, 0:128] + (wide[:, 128:] + dot(lo_ref[...], vh))


def lower_mask(d):
    i = lax.broadcasted_iota(jnp.int32, d.shape, 0)
    j = lax.broadcasted_iota(jnp.int32, d.shape, 1)
    return jnp.where(i > j, d, 0.0)


def upper_mask(d):
    i = lax.broadcasted_iota(jnp.int32, d.shape, 0)
    j = lax.broadcasted_iota(jnp.int32, d.shape, 1)
    return jnp.where(i <= j, d, 0.0)


def start_kernel(ids, b_ref, d_ref, after_ref, y_ref, yb_ref, lh_ref, ll_ref, *uppers):
    lh_ref[...], ll_ref[...] = split(lower_mask(d_ref[ids[2]]))
    w = b_ref[...]
    y = w + apply(lh_ref, ll_ref, w)
    y_ref[...] = y
    yb_ref[...] = y.astype(BF16)
    for n, j in enumerate((ids[2], 1, 2)):
        uppers[2 * n][...], uppers[2 * n + 1][...] = split(upper_mask(d_ref[j]))


def combine_kernel(ids, own_ref, r1, r2, r3, v_ref):
    v_ref[...] = own_or_received(ids, 0, own_ref, (r1, r2, r3))


def own_or_received(ids, j, own_ref, received):
    if not received:
        return own_ref[...]
    total = received[0][...]
    for piece in received[1:]:
        total = total + piece[...]
    return jnp.where(ids[2] == j, own_ref[...], total)


def window_blocks(blocks, d):
    return blocks[d], (blocks[4] if d == 0 else blocks[5].at[(d - 1) * NB : d * NB, :])


def block_product(ids, blocks, j, v_ref, acc_ref):
    x, h = ids[0], ids[1]
    for d in range(NX):
        @pl.when(lax.rem(x + d, NX) == j)
        def _():
            same, other = window_blocks(blocks, d)
            acc_ref[...] -= dot(same[...], v_ref[pl.ds(pl.multiple_of(h * HB, HB), HB), :]) + dot(
                other[...], v_ref[pl.ds(pl.multiple_of((1 - h) * HB, HB), HB), :]
            )


def forward_kernel(j, count, ids, w_ref, own_ref, prior_ref, lh_ref, ll_ref, *rest):
    blocks, received, (v_ref, w_out, y_ref, yb_ref) = rest[:6], rest[6 : 6 + count], rest[-4:]
    v_ref[...] = own_or_received(ids, j, own_ref, received)
    w_out[...] = w_ref[...]
    block_product(ids, blocks, j, v_ref, w_out)
    w = w_out[...]
    y = w + apply(lh_ref, ll_ref, w)
    y_ref[...] = jnp.where(ids[2] == j + 1, y, prior_ref[...])
    if j == 0:
        yb_ref[...] = y.astype(BF16)
    else:
        yb_ref[0:NB, :] = v_ref[...]
        yb_ref[NB:, :] = y.astype(BF16)


def pick_kernel(ids, b0, b1, b2, b3, p23_ref, p1_ref, all_ref):
    for d, block in enumerate((b1, b2, b3)):
        all_ref[d * NB : (d + 1) * NB, :] = block[...]
    for d, block in enumerate((b0, b1, b2, b3)):
        @pl.when(lax.rem(ids[0] + d, NX) == 2)
        def _():
            p1_ref[:, 0:HB] = block[...]

        @pl.when(lax.rem(ids[0] + d, NX) == 3)
        def _():
            p23_ref[...] = block[...]
            p1_ref[:, HB:] = block[...]


def relay_kernel(ids, p23_ref, p1_ref, after_ref, q23_ref, q1_ref):
    q23_ref[...] = p23_ref[...]
    q1_ref[...] = p1_ref[...]


def turn_kernel(
    ids, w_ref, y12_ref, y12_in, prior_ref, lh, ll, u3h, u3l, u1h, u1l, u2h, u2l, p23, p23_other, p1, p1_other, *rest
):
    blocks, (y1_ref, y2_ref, y_ref, yb_ref, x_ref, x23_ref, x3_ref, acc) = rest[:6], rest[-8:]
    h = ids[1]
    last = ids[2] == 3
    y1_ref[...] = jnp.where(last, y12_in[0:NB, :], y12_ref[0:NB, :])
    y2 = jnp.where(last, y12_in[NB:, :], y12_ref[NB:, :])
    y2_ref[...] = y2
    acc[...] = w_ref[...]
    block_product(ids, blocks, 1, y1_ref, acc)
    block_product(ids, blocks, 2, y2_ref, acc)
    w = acc[...]
    y3 = w + apply(lh, ll, w)
    y_ref[...] = jnp.where(ids[2] == 3, y3, prior_ref[...])
    yb_ref[...] = y3.astype(BF16)

    def product(same, other, row):
        return dot(same, x_ref[pl.ds(pl.multiple_of(row + h * HB, HB), HB), :]) + dot(
            other, x_ref[pl.ds(pl.multiple_of(row + (1 - h) * HB, HB), HB), :]
        )

    x3 = apply(u3h, u3l, y3).astype(BF16)
    x_ref[2 * NB :, :] = x3
    x23_ref[NB:, :] = x3
    x3_ref[...] = x3
    t = y2.astype(F32) - product(p23[...], p23_other[...], 2 * NB)
    x2 = apply(u2h, u2l, t).astype(BF16)
    x_ref[NB : 2 * NB, :] = x2
    x23_ref[0:NB, :] = x2
    t = y1_ref[...].astype(F32) - product(p1[:, 0:HB], p1_other[:, 0:HB], NB) - product(p1[:, HB:], p1_other[:, HB:], 2 * NB)
    x_ref[0:NB, :] = apply(u1h, u1l, t).astype(BF16)


def hold_kernel(ids, top, bottom, *rest):
    top_out, bottom_out = rest[-2:]
    top_out[...] = top[...]
    bottom_out[...] = bottom[...]


def late_kernel(ids, to0, to1, to2, y1, y2, y3, *rest):
    late_ref, z = rest[-1], ids[2]
    late_ref[0:NB, :] = jnp.where(z >= 1, y1[...], to0[0:NB, :])
    late_ref[NB : 2 * NB, :] = jnp.where(z >= 2, y2[...], to0[NB : 2 * NB, :] + to1[0:NB, :])
    late_ref[2 * NB :, :] = jnp.where(z >= 3, y3[...], to0[2 * NB :, :] + to1[NB:, :] + to2[...])


def unknowns_kernel(ids, v0, e1, e2, e3, late, s1, s2, s3, v_ref, mine_ref, theirs_ref):
    h, owner = ids[1], ids[3] == 0
    v_ref[0:NB, :] = jnp.where(owner, v0[...], e1[...] + e2[...] + e3[...])
    v_ref[NB:, :] = jnp.where(owner, late[...], s1[...] + s2[...] + s3[...])
    for j in range(4):
        rows = slice(j * HB, (j + 1) * HB)
        mine_ref[rows, :] = v_ref[pl.ds(pl.multiple_of(j * NB + h * HB, HB), HB), :]
        theirs_ref[rows, :] = v_ref[pl.ds(pl.multiple_of(j * NB + (1 - h) * HB, HB), HB), :]


def window_kernel(ids, b_ref, v_ref, own_ref, uh_ref, ul_ref, *rest):
    blocks, (out_ref, acc) = rest[:6], rest[6:]
    x, h, z, owner = ids[0], ids[1], ids[2], ids[3] == 0
    acc[...] = jnp.where(owner, own_ref[...], b_ref[...])
    for d in range(NX):
        j = lax.rem(x + d, NX)
        for s in range(2):
            part = h if s == 0 else 1 - h

            @pl.when(jnp.logical_or(jnp.logical_not(owner), j > z))
            def _():
                block = window_blocks(blocks, d)[s]
                acc[...] -= dot(block[...], v_ref[pl.ds(pl.multiple_of(j * NB + part * HB, HB), HB), :])

    @pl.when(owner)
    def _():
        out_ref[...] = apply(uh_ref, ul_ref, acc[...])

    @pl.when(jnp.logical_not(owner))
    def _():
        out_ref[...] = acc[...]


def rows_kernel(tiles, ids, mine_ref, other_ref, *rest):
    blocks, (own_ref, part_ref, v_ref) = rest[:4], rest[4:]
    v_ref[:, 0:128] = mine_ref[...]
    v_ref[:, 128:] = other_ref[...]
    tile = own_ref.shape[0] // tiles
    for t in range(tiles):
        rows = slice(t * tile, (t + 1) * tile)
        total = None
        for d in range(NX):
            j = lax.rem(ids[0] + d, NX)
            term = dot(blocks[d][rows, :], v_ref[pl.ds(pl.multiple_of(j * HB, HB), HB), :])
            total = term if total is None else total + term
        own_ref[rows, :] = total[:, 0:128]
        part_ref[rows, :] = total[:, 128:].astype(BF16)


def add_kernel(ids, out_in, b_ref, own_t, part_t, own_b, part_b, out_ref):
    i, n = pl.program_id(0), out_ref.shape[0]
    half = own_t.shape[0] // n
    for top, own, part in ((True, own_t, part_t), (False, own_b, part_b)):
        @pl.when((i < half) == top)
        def _():
            rows = pl.ds(pl.multiple_of((i if top else i - half) * n, n), n)
            base = b_ref[pl.ds(pl.multiple_of(NB + i * n, 128), n), :]
            out_ref[...] = base - own[rows, :] - part[rows, :].astype(F32)


def whole(shape):
    return pl.BlockSpec(memory_space=pltpu.VMEM)


def in_hbm(a):
    return pltpu.with_memory_space_constraint(a, pltpu.HBM)


ANY = pl.BlockSpec(memory_space=pl.ANY)


def call(kernel, ids, args, specs, outs, scratch=(), grid=(1,), out_spec=None, limit=12, aliases={}):
    out_specs = jax.tree.map(lambda o: whole(o.shape), outs) if out_spec is None else out_spec
    return pl.pallas_call(
        kernel,
        grid_spec=pltpu.PrefetchScalarGridSpec(
            num_scalar_prefetch=1, grid=grid, in_specs=specs, out_specs=out_specs, scratch_shapes=scratch
        ),
        out_shape=outs,
        input_output_aliases=aliases,
        cost_estimate=pl.CostEstimate(flops=1, bytes_accessed=1, transcendentals=0),
        compiler_params=pltpu.CompilerParams(vmem_limit_bytes=limit * 1024 * 1024),
    )(ids, *args)


def body(rhs, factors, diag_inv):
    rows, cols = rhs.shape
    r, c = lax.axis_index("row"), lax.axis_index("col")
    ids = jnp.stack([r // NH, r % NH, c // NY, c % NY]).astype(jnp.int32)

    def bf(n, width=cols):
        return jax.ShapeDtypeStruct((n, width), BF16)

    vec, mat = jax.ShapeDtypeStruct((NB, cols), F32), bf(NB, NB)
    vspec, mspec = whole((NB, cols)), whole((NB, NB))
    first = pl.BlockSpec((NB, cols), lambda i, ids: (0, 0))

    own = factors[:NB]
    same = [own, send(own, x_minus), send(own, x_far), send(own, x_plus)]
    half = (rows - NB) // 2
    own_t, own_b = factors[NB : NB + half], factors[NB + half :]
    own_other = send(own, other_core)
    wspecs = [whole((NB, HB))] * 6

    y_z0, yb0, lh, ll, *uppers = call(
        start_kernel, ids, (in_hbm(rhs), in_hbm(diag_inv), own), [first, pl.BlockSpec((4, NB, NB), lambda i, ids: (0, 0, 0)), ANY],
        (vec, bf(NB), mat, mat) + (mat,) * 6, limit=16,
    )
    hops = [send(yb0, z_move(0, t)) for t in (1, 2, 3)]
    p23, p1, received = call(
        pick_kernel, ids, same, [whole((NB, HB))] * 4, (bf(NB, HB), bf(NB, 2 * HB), bf(3 * NB, HB))
    )
    window = [*same, own_other, send(received, other_core)]
    p23 = send(p23, z_move(2, 3))
    p1 = send(p1, z_move(1, 3))

    def forward(j, w, wspec, own, prior, received, after=()):
        return call(
            functools.partial(forward_kernel, j, len(received)), ids, (w, own, prior, lh, ll, *window, *received, *after),
            [wspec, vspec, vspec, mspec, mspec, *wspecs] + [vspec] * len(received) + [ANY] * len(after), (bf(NB), vec, vec, bf(NB if j == 0 else 2 * NB)),
        )

    y0 = call(combine_kernel, ids, (yb0, *hops), [vspec] * 4, bf(NB))
    early = [send(y0, y_move(t)) for t in (1, 2, 3)]
    top, bottom = call(
        hold_kernel, ids, (own_t, own_b, *early, window[5]), [whole((half, HB))] * 2 + [ANY] * 4, (bf(half, HB),) * 2
    )
    before_t, after_b = send(top, x_plus), send(bottom, x_minus)
    far_t, far_b = send(before_t, x_plus), send(after_b, x_minus)
    _, w0, y_own, yb1 = forward(0, in_hbm(rhs), first, y0, y_z0, ())
    hops = [send(yb1, z_move(1, 2))]
    _, _, y_own, y12 = forward(1, w0, vspec, yb1, y_own, hops)
    y12_in = send(y12, z_move(2, 3))
    top, bottom = call(hold_kernel, ids, (own_t, own_b, y12_in), [whole((half, HB))] * 2 + [ANY], (bf(half, HB),) * 2)
    before_b, after_t = send(bottom, x_plus), send(top, x_minus)
    p23, p1 = call(relay_kernel, ids, (p23, p1, y12), [whole((NB, HB)), mspec, ANY], (bf(NB, HB), bf(NB, 2 * HB)))
    p23_other, p1_other = send(p23, other_core), send(p1, other_core)
    y1, y2, y_own, yb3, xs, x23s, x3s = call(
        turn_kernel, ids,
        (w0, y12, y12_in, y_own, lh, ll, *uppers, p23, p23_other, p1, p1_other, *window, before_t, after_b),
        [vspec] * 4 + [mspec] * 8 + [whole((NB, HB))] * 2 + [mspec] * 2 + wspecs + [ANY] * 2,
        (bf(NB), bf(NB), vec, bf(NB), bf(3 * NB), bf(2 * NB), bf(NB)), scratch=[pltpu.VMEM((NB, cols), F32)],
    )
    to0, to1, to2 = send(xs, z_move(3, 0)), send(x23s, z_move(3, 1)), send(x3s, z_move(3, 2))
    late = call(
        late_kernel, ids, (to0, to1, to2, y1, y2, yb3, before_b, after_t),
        [whole((3 * NB, cols)), whole((2 * NB, cols))] + [vspec] * 4 + [ANY] * 2, bf(3 * NB),
    )
    spread = [send(late, y_move(t)) for t in (1, 2, 3)]
    out = jax.ShapeDtypeStruct((rows, cols), F32)
    v, mine, theirs = call(
        unknowns_kernel, ids, (y0, *early, late, *spread), [vspec] * 4 + [whole((3 * NB, cols))] * 4,
        (bf(4 * NB), bf(4 * HB), bf(4 * HB)),
    )
    other = send(theirs, other_core)
    done = call(
        window_kernel, ids, (in_hbm(rhs), v, y_own, uppers[0], uppers[1], *window),
        [first, whole((4 * NB, cols)), vspec, mspec, mspec, *wspecs], out, out_spec=first, scratch=[pltpu.VMEM((NB, cols), F32)],
    )
    sums, parts = [], []
    for blocks in ((own_t, after_t, far_t, before_t), (own_b, after_b, far_b, before_b)):
        total, part = call(
            functools.partial(rows_kernel, 2), ids, (mine, other, *blocks),
            [vspec] * 2 + [mspec] * 4, (jax.ShapeDtypeStruct((half, cols), F32), bf(half)),
            scratch=[pltpu.VMEM((4 * HB, 2 * cols), BF16)], limit=24,
        )
        sums.append(total)
        parts.append(send(part, other_core))
    tile = half // 2
    at = pl.BlockSpec((pl.Element(tile), pl.Element(cols)), lambda i, ids: (pl.multiple_of(NB + i * tile, 128), 0))
    return call(
        add_kernel, ids, (done, rhs, sums[0], parts[0], sums[1], parts[1]),
        [ANY] + [vspec] * 5, out, grid=(4,), out_spec=at, aliases={1: 0},
    )


def solution(mesh):
    placed = (P("col", "row"), P("col", "row"), P())
    return jax.shard_map(body, mesh=mesh, in_specs=placed, out_specs=P("col", "row"), check_vma=False)
```

```python
import functools

import jax
import jax.numpy as jnp
from jax import lax
from jax.experimental import pallas as pl
from jax.experimental.pallas import tpu as pltpu
from jax.sharding import PartitionSpec as P

NX, NH, NZ, NY = 4, 2, 4, 4
NB = 512
HB = 256
F32, BF16 = jnp.float32, jnp.bfloat16


def pairs(move):
    out = []
    for r in range(NX * NH):
        for c in range(NZ * NY):
            x, h = divmod(r, NH)
            z, y = divmod(c, NY)
            to = move(x, h, z, y)
            if to is not None:
                x2, h2, z2, y2 = to
                out.append((r * NZ * NY + c, ((x2 % NX) * NH + h2 % NH) * NZ * NY + (z2 % NZ) * NY + y2 % NY))
    return out


def send(value, move):
    return lax.ppermute(value, ("row", "col"), pairs(move))


def x_plus(x, h, z, y):
    return (x + 1, h, z, y)


def x_minus(x, h, z, y):
    return (x - 1, h, z, y)


def x_far(x, h, z, y):
    return (x + 2, h, z, y)


def other_core(x, h, z, y):
    return (x, 1 - h, z, y)


def z_move(src, dst):
    return lambda x, h, z, y: (x, h, dst, y) if (y == 0 and z == src) else None


def y_move(step):
    return lambda x, h, z, y: (x, h, z, step) if y == 0 else None


def dot(a, b):
    return jnp.dot(a, b, preferred_element_type=F32)


def split(a):
    hi = a.astype(BF16)
    return hi, (a - hi.astype(F32)).astype(BF16)


def apply(hi_ref, lo_ref, v):
    vh, vl = split(v)
    wide = dot(hi_ref[...], jnp.concatenate([vh, vl], axis=1))
    return wide[:, 0:128] + (wide[:, 128:] + dot(lo_ref[...], vh))


def lower_mask(d):
    i = lax.broadcasted_iota(jnp.int32, d.shape, 0)
    j = lax.broadcasted_iota(jnp.int32, d.shape, 1)
    return jnp.where(i > j, d, 0.0)


def upper_mask(d):
    i = lax.broadcasted_iota(jnp.int32, d.shape, 0)
    j = lax.broadcasted_iota(jnp.int32, d.shape, 1)
    return jnp.where(i <= j, d, 0.0)


def start_kernel(ids, b_ref, d_ref, after_ref, y_ref, yb_ref, lh_ref, ll_ref, *uppers):
    lh_ref[...], ll_ref[...] = split(lower_mask(d_ref[ids[2]]))
    w = b_ref[...]
    y = w + apply(lh_ref, ll_ref, w)
    y_ref[...] = y
    yb_ref[...] = y.astype(BF16)
    for n, j in enumerate((ids[2], 1, 2)):
        uppers[2 * n][...], uppers[2 * n + 1][...] = split(upper_mask(d_ref[j]))


def combine_kernel(ids, own_ref, r1, r2, r3, v_ref):
    v_ref[...] = own_or_received(ids, 0, own_ref, (r1, r2, r3))


def own_or_received(ids, j, own_ref, received):
    if not received:
        return own_ref[...]
    total = received[0][...]
    for piece in received[1:]:
        total = total + piece[...]
    return jnp.where(ids[2] == j, own_ref[...], total)


def window_blocks(blocks, d):
    return blocks[d], (blocks[4] if d == 0 else blocks[5].at[(d - 1) * NB : d * NB, :])


def block_product(ids, blocks, j, v_ref, acc_ref):
    x, h = ids[0], ids[1]
    for d in range(NX):
        @pl.when(lax.rem(x + d, NX) == j)
        def _():
            same, other = window_blocks(blocks, d)
            acc_ref[...] -= dot(same[...], v_ref[pl.ds(pl.multiple_of(h * HB, HB), HB), :]) + dot(
                other[...], v_ref[pl.ds(pl.multiple_of((1 - h) * HB, HB), HB), :]
            )


def forward_kernel(j, count, ids, w_ref, own_ref, prior_ref, lh_ref, ll_ref, *rest):
    blocks, received, (v_ref, w_out, y_ref, yb_ref) = rest[:6], rest[6 : 6 + count], rest[-4:]
    v_ref[...] = own_or_received(ids, j, own_ref, received)
    w_out[...] = w_ref[...]
    block_product(ids, blocks, j, v_ref, w_out)
    w = w_out[...]
    y = w + apply(lh_ref, ll_ref, w)
    y_ref[...] = jnp.where(ids[2] == j + 1, y, prior_ref[...])
    if j == 0:
        yb_ref[...] = y.astype(BF16)
    else:
        yb_ref[0:NB, :] = v_ref[...]
        yb_ref[NB:, :] = y.astype(BF16)


def pick_kernel(ids, b0, b1, b2, b3, p23_ref, p1_ref, all_ref):
    for d, block in enumerate((b1, b2, b3)):
        all_ref[d * NB : (d + 1) * NB, :] = block[...]
    for d, block in enumerate((b0, b1, b2, b3)):
        @pl.when(lax.rem(ids[0] + d, NX) == 2)
        def _():
            p1_ref[:, 0:HB] = block[...]

        @pl.when(lax.rem(ids[0] + d, NX) == 3)
        def _():
            p23_ref[...] = block[...]
            p1_ref[:, HB:] = block[...]


def relay_kernel(ids, p23_ref, p1_ref, after_ref, q23_ref, q1_ref):
    q23_ref[...] = p23_ref[...]
    q1_ref[...] = p1_ref[...]


def turn_kernel(
    ids, w_ref, y12_ref, y12_in, prior_ref, lh, ll, u3h, u3l, u1h, u1l, u2h, u2l, p23, p23_other, p1, p1_other, *rest
):
    blocks, (y1_ref, y2_ref, y_ref, yb_ref, x_ref, x23_ref, x3_ref, acc) = rest[:6], rest[-8:]
    h = ids[1]
    last = ids[2] == 3
    y1_ref[...] = jnp.where(last, y12_in[0:NB, :], y12_ref[0:NB, :])
    y2 = jnp.where(last, y12_in[NB:, :], y12_ref[NB:, :])
    y2_ref[...] = y2
    acc[...] = w_ref[...]
    block_product(ids, blocks, 1, y1_ref, acc)
    block_product(ids, blocks, 2, y2_ref, acc)
    w = acc[...]
    y3 = w + apply(lh, ll, w)
    y_ref[...] = jnp.where(ids[2] == 3, y3, prior_ref[...])
    yb_ref[...] = y3.astype(BF16)

    def product(same, other, row):
        return dot(same, x_ref[pl.ds(pl.multiple_of(row + h * HB, HB), HB), :]) + dot(
            other, x_ref[pl.ds(pl.multiple_of(row + (1 - h) * HB, HB), HB), :]
        )

    x3 = apply(u3h, u3l, y3).astype(BF16)
    x_ref[2 * NB :, :] = x3
    x23_ref[NB:, :] = x3
    x3_ref[...] = x3
    t = y2.astype(F32) - product(p23[...], p23_other[...], 2 * NB)
    x2 = apply(u2h, u2l, t).astype(BF16)
    x_ref[NB : 2 * NB, :] = x2
    x23_ref[0:NB, :] = x2
    t = y1_ref[...].astype(F32) - product(p1[:, 0:HB], p1_other[:, 0:HB], NB) - product(p1[:, HB:], p1_other[:, HB:], 2 * NB)
    x_ref[0:NB, :] = apply(u1h, u1l, t).astype(BF16)


def hold_kernel(ids, top, bottom, *rest):
    top_out, bottom_out = rest[-2:]
    top_out[...] = top[...]
    bottom_out[...] = bottom[...]


def late_kernel(ids, to0, to1, to2, y1, y2, y3, *rest):
    late_ref, z = rest[-1], ids[2]
    late_ref[0:NB, :] = jnp.where(z >= 1, y1[...], to0[0:NB, :])
    late_ref[NB : 2 * NB, :] = jnp.where(z >= 2, y2[...], to0[NB : 2 * NB, :] + to1[0:NB, :])
    late_ref[2 * NB :, :] = jnp.where(z >= 3, y3[...], to0[2 * NB :, :] + to1[NB:, :] + to2[...])


def unknowns_kernel(ids, v0, e1, e2, e3, late, s1, s2, s3, v_ref, mine_ref, theirs_ref):
    h, owner = ids[1], ids[3] == 0
    v_ref[0:NB, :] = jnp.where(owner, v0[...], e1[...] + e2[...] + e3[...])
    v_ref[NB:, :] = jnp.where(owner, late[...], s1[...] + s2[...] + s3[...])
    for j in range(4):
        rows = slice(j * HB, (j + 1) * HB)
        mine_ref[rows, :] = v_ref[pl.ds(pl.multiple_of(j * NB + h * HB, HB), HB), :]
        theirs_ref[rows, :] = v_ref[pl.ds(pl.multiple_of(j * NB + (1 - h) * HB, HB), HB), :]


def window_kernel(ids, b_ref, v_ref, own_ref, uh_ref, ul_ref, *rest):
    blocks, (out_ref, acc) = rest[:6], rest[6:]
    x, h, z, owner = ids[0], ids[1], ids[2], ids[3] == 0
    acc[...] = jnp.where(owner, own_ref[...], b_ref[...])
    for d in range(NX):
        j = lax.rem(x + d, NX)
        for s in range(2):
            part = h if s == 0 else 1 - h

            @pl.when(jnp.logical_or(jnp.logical_not(owner), j > z))
            def _():
                block = window_blocks(blocks, d)[s]
                acc[...] -= dot(block[...], v_ref[pl.ds(pl.multiple_of(j * NB + part * HB, HB), HB), :])

    @pl.when(owner)
    def _():
        out_ref[...] = apply(uh_ref, ul_ref, acc[...])

    @pl.when(jnp.logical_not(owner))
    def _():
        out_ref[...] = acc[...]


def rows_kernel(tiles, ids, mine_ref, other_ref, *rest):
    blocks, (own_ref, part_ref, v_ref) = rest[:4], rest[4:]
    v_ref[:, 0:128] = mine_ref[...]
    v_ref[:, 128:] = other_ref[...]
    tile = own_ref.shape[0] // tiles
    for t in range(tiles):
        rows = slice(t * tile, (t + 1) * tile)
        total = None
        for d in range(NX):
            j = lax.rem(ids[0] + d, NX)
            term = dot(blocks[d][rows, :], v_ref[pl.ds(pl.multiple_of(j * HB, HB), HB), :])
            total = term if total is None else total + term
        own_ref[rows, :] = total[:, 0:128]
        part_ref[rows, :] = total[:, 128:].astype(BF16)


def add_kernel(ids, out_in, b_ref, own_t, part_t, own_b, part_b, out_ref):
    i, n = pl.program_id(0), out_ref.shape[0]
    half = own_t.shape[0] // n
    for top, own, part in ((True, own_t, part_t), (False, own_b, part_b)):
        @pl.when((i < half) == top)
        def _():
            rows = pl.ds(pl.multiple_of((i if top else i - half) * n, n), n)
            base = b_ref[pl.ds(pl.multiple_of(NB + i * n, 128), n), :]
            out_ref[...] = base - own[rows, :] - part[rows, :].astype(F32)


def whole(shape):
    return pl.BlockSpec(memory_space=pltpu.VMEM)


def in_hbm(a):
    return pltpu.with_memory_space_constraint(a, pltpu.HBM)


ANY = pl.BlockSpec(memory_space=pl.ANY)


def call(kernel, ids, args, specs, outs, scratch=(), grid=(1,), out_spec=None, limit=12, aliases={}):
    out_specs = jax.tree.map(lambda o: whole(o.shape), outs) if out_spec is None else out_spec
    return pl.pallas_call(
        kernel,
        grid_spec=pltpu.PrefetchScalarGridSpec(
            num_scalar_prefetch=1, grid=grid, in_specs=specs, out_specs=out_specs, scratch_shapes=scratch
        ),
        out_shape=outs,
        input_output_aliases=aliases,
        cost_estimate=pl.CostEstimate(flops=1, bytes_accessed=1, transcendentals=0),
        compiler_params=pltpu.CompilerParams(vmem_limit_bytes=limit * 1024 * 1024),
    )(ids, *args)


def body(rhs, factors, diag_inv):
    rows, cols = rhs.shape
    r, c = lax.axis_index("row"), lax.axis_index("col")
    ids = jnp.stack([r // NH, r % NH, c // NY, c % NY]).astype(jnp.int32)

    def bf(n, width=cols):
        return jax.ShapeDtypeStruct((n, width), BF16)

    vec, mat = jax.ShapeDtypeStruct((NB, cols), F32), bf(NB, NB)
    vspec, mspec = whole((NB, cols)), whole((NB, NB))
    first = pl.BlockSpec((NB, cols), lambda i, ids: (0, 0))

    own = factors[:NB]
    same = [own, send(own, x_minus), send(own, x_far), send(own, x_plus)]
    half = (rows - NB) // 2
    own_t, own_b = factors[NB : NB + half], factors[NB + half :]
    own_other = send(own, other_core)
    wspecs = [whole((NB, HB))] * 6

    y_z0, yb0, lh, ll, *uppers = call(
        start_kernel, ids, (in_hbm(rhs), in_hbm(diag_inv), own), [first, pl.BlockSpec((4, NB, NB), lambda i, ids: (0, 0, 0)), ANY],
        (vec, bf(NB), mat, mat) + (mat,) * 6, limit=16,
    )
    hops = [send(yb0, z_move(0, t)) for t in (1, 2, 3)]
    p23, p1, received = call(
        pick_kernel, ids, same, [whole((NB, HB))] * 4, (bf(NB, HB), bf(NB, 2 * HB), bf(3 * NB, HB))
    )
    window = [*same, own_other, send(received, other_core)]
    p23 = send(p23, z_move(2, 3))
    p1 = send(p1, z_move(1, 3))

    def forward(j, w, wspec, own, prior, received, after=()):
        return call(
            functools.partial(forward_kernel, j, len(received)), ids, (w, own, prior, lh, ll, *window, *received, *after),
            [wspec, vspec, vspec, mspec, mspec, *wspecs] + [vspec] * len(received) + [ANY] * len(after), (bf(NB), vec, vec, bf(NB if j == 0 else 2 * NB)),
        )

    y0 = call(combine_kernel, ids, (yb0, *hops), [vspec] * 4, bf(NB))
    early = [send(y0, y_move(t)) for t in (1, 2, 3)]
    top, bottom = call(
        hold_kernel, ids, (own_t, own_b, *hops), [whole((half, HB))] * 2 + [ANY] * 3, (bf(half, HB),) * 2
    )
    before_t, after_b = send(top, x_plus), send(bottom, x_minus)
    far_t, far_b = send(before_t, x_plus), send(after_b, x_minus)
    _, w0, y_own, yb1 = forward(0, in_hbm(rhs), first, y0, y_z0, (), early)
    hops = [send(yb1, z_move(1, 2))]
    _, _, y_own, y12 = forward(1, w0, vspec, yb1, y_own, hops)
    y12_in = send(y12, z_move(2, 3))
    before_b, after_t = send(bottom, x_plus), send(top, x_minus)
    p23, p1 = call(relay_kernel, ids, (p23, p1, y12), [whole((NB, HB)), mspec, ANY], (bf(NB, HB), bf(NB, 2 * HB)))
    p23_other, p1_other = send(p23, other_core), send(p1, other_core)
    y1, y2, y_own, yb3, xs, x23s, x3s = call(
        turn_kernel, ids,
        (w0, y12, y12_in, y_own, lh, ll, *uppers, p23, p23_other, p1, p1_other, *window, before_t, after_b),
        [vspec] * 4 + [mspec] * 8 + [whole((NB, HB))] * 2 + [mspec] * 2 + wspecs + [ANY] * 2,
        (bf(NB), bf(NB), vec, bf(NB), bf(3 * NB), bf(2 * NB), bf(NB)), scratch=[pltpu.VMEM((NB, cols), F32)],
    )
    to0, to1, to2 = send(xs, z_move(3, 0)), send(x23s, z_move(3, 1)), send(x3s, z_move(3, 2))
    late = call(
        late_kernel, ids, (to0, to1, to2, y1, y2, yb3, before_b, after_t),
        [whole((3 * NB, cols)), whole((2 * NB, cols))] + [vspec] * 4 + [ANY] * 2, bf(3 * NB),
    )
    spread = [send(late, y_move(t)) for t in (1, 2, 3)]
    out = jax.ShapeDtypeStruct((rows, cols), F32)
    v, mine, theirs = call(
        unknowns_kernel, ids, (y0, *early, late, *spread), [vspec] * 4 + [whole((3 * NB, cols))] * 4,
        (bf(4 * NB), bf(4 * HB), bf(4 * HB)),
    )
    other = send(theirs, other_core)
    done = call(
        window_kernel, ids, (in_hbm(rhs), v, y_own, uppers[0], uppers[1], *window),
        [first, whole((4 * NB, cols)), vspec, mspec, mspec, *wspecs], out, out_spec=first, scratch=[pltpu.VMEM((NB, cols), F32)],
    )
    sums, parts = [], []
    for blocks in ((own_t, after_t, far_t, before_t), (own_b, after_b, far_b, before_b)):
        total, part = call(
            functools.partial(rows_kernel, 2), ids, (mine, other, *blocks),
            [vspec] * 2 + [mspec] * 4, (jax.ShapeDtypeStruct((half, cols), F32), bf(half)),
            scratch=[pltpu.VMEM((4 * HB, 2 * cols), BF16)], limit=24,
        )
        sums.append(total)
        parts.append(send(part, other_core))
    tile = half // 2
    at = pl.BlockSpec((pl.Element(tile), pl.Element(cols)), lambda i, ids: (pl.multiple_of(NB + i * tile, 128), 0))
    return call(
        add_kernel, ids, (done, rhs, sums[0], parts[0], sums[1], parts[1]),
        [ANY] + [vspec] * 5, out, grid=(4,), out_spec=at, aliases={1: 0},
    )


def solution(mesh):
    placed = (P("col", "row"), P("col", "row"), P())
    return jax.shard_map(body, mesh=mesh, in_specs=placed, out_specs=P("col", "row"), check_vma=False)
```

```python
import functools

import jax
import jax.numpy as jnp
from jax import lax
from jax.experimental import pallas as pl
from jax.experimental.pallas import tpu as pltpu
from jax.sharding import PartitionSpec as P

NX, NH, NZ, NY = 4, 2, 4, 4
NB = 512
HB = 256
F32, BF16 = jnp.float32, jnp.bfloat16


def pairs(move):
    out = []
    for r in range(NX * NH):
        for c in range(NZ * NY):
            x, h = divmod(r, NH)
            z, y = divmod(c, NY)
            to = move(x, h, z, y)
            if to is not None:
                x2, h2, z2, y2 = to
                out.append((r * NZ * NY + c, ((x2 % NX) * NH + h2 % NH) * NZ * NY + (z2 % NZ) * NY + y2 % NY))
    return out


def send(value, move):
    return lax.ppermute(value, ("row", "col"), pairs(move))


def x_plus(x, h, z, y):
    return (x + 1, h, z, y)


def x_minus(x, h, z, y):
    return (x - 1, h, z, y)


def x_far(x, h, z, y):
    return (x + 2, h, z, y)


def other_core(x, h, z, y):
    return (x, 1 - h, z, y)


def z_move(src, dst):
    return lambda x, h, z, y: (x, h, dst, y) if (y == 0 and z == src) else None


def y_move(step):
    return lambda x, h, z, y: (x, h, z, step) if y == 0 else None


def dot(a, b):
    return jnp.dot(a, b, preferred_element_type=F32)


def split(a):
    hi = a.astype(BF16)
    return hi, (a - hi.astype(F32)).astype(BF16)


def apply(hi_ref, lo_ref, v):
    vh, vl = split(v)
    wide = dot(hi_ref[...], jnp.concatenate([vh, vl], axis=1))
    return wide[:, 0:128] + (wide[:, 128:] + dot(lo_ref[...], vh))


def lower_mask(d):
    i = lax.broadcasted_iota(jnp.int32, d.shape, 0)
    j = lax.broadcasted_iota(jnp.int32, d.shape, 1)
    return jnp.where(i > j, d, 0.0)


def upper_mask(d):
    i = lax.broadcasted_iota(jnp.int32, d.shape, 0)
    j = lax.broadcasted_iota(jnp.int32, d.shape, 1)
    return jnp.where(i <= j, d, 0.0)


def start_kernel(ids, b_ref, d_ref, after_ref, y_ref, yb_ref, lh_ref, ll_ref, *uppers):
    lh_ref[...], ll_ref[...] = split(lower_mask(d_ref[ids[2]]))
    w = b_ref[...]
    y = w + apply(lh_ref, ll_ref, w)
    y_ref[...] = y
    yb_ref[...] = y.astype(BF16)
    for n, j in enumerate((ids[2], 1, 2)):
        uppers[2 * n][...], uppers[2 * n + 1][...] = split(upper_mask(d_ref[j]))


def combine_kernel(ids, own_ref, r1, r2, r3, v_ref):
    v_ref[...] = own_or_received(ids, 0, own_ref, (r1, r2, r3))


def own_or_received(ids, j, own_ref, received):
    if not received:
        return own_ref[...]
    total = received[0][...]
    for piece in received[1:]:
        total = total + piece[...]
    return jnp.where(ids[2] == j, own_ref[...], total)


def window_blocks(blocks, d):
    return blocks[d], (blocks[4] if d == 0 else blocks[5].at[(d - 1) * NB : d * NB, :])


def block_product(ids, blocks, j, v_ref, acc_ref):
    x, h = ids[0], ids[1]
    for d in range(NX):
        @pl.when(lax.rem(x + d, NX) == j)
        def _():
            same, other = window_blocks(blocks, d)
            acc_ref[...] -= dot(same[...], v_ref[pl.ds(pl.multiple_of(h * HB, HB), HB), :]) + dot(
                other[...], v_ref[pl.ds(pl.multiple_of((1 - h) * HB, HB), HB), :]
            )


def forward_kernel(j, count, ids, w_ref, own_ref, prior_ref, lh_ref, ll_ref, *rest):
    blocks, received, (v_ref, w_out, y_ref, yb_ref) = rest[:6], rest[6 : 6 + count], rest[-4:]
    v_ref[...] = own_or_received(ids, j, own_ref, received)
    w_out[...] = w_ref[...]
    block_product(ids, blocks, j, v_ref, w_out)
    w = w_out[...]
    y = w + apply(lh_ref, ll_ref, w)
    y_ref[...] = jnp.where(ids[2] == j + 1, y, prior_ref[...])
    if j == 0:
        yb_ref[...] = y.astype(BF16)
    else:
        yb_ref[0:NB, :] = v_ref[...]
        yb_ref[NB:, :] = y.astype(BF16)


def pick_kernel(ids, b0, b1, b2, b3, p23_ref, p1_ref, all_ref):
    for d, block in enumerate((b1, b2, b3)):
        all_ref[d * NB : (d + 1) * NB, :] = block[...]
    for d, block in enumerate((b0, b1, b2, b3)):
        @pl.when(lax.rem(ids[0] + d, NX) == 2)
        def _():
            p1_ref[:, 0:HB] = block[...]

        @pl.when(lax.rem(ids[0] + d, NX) == 3)
        def _():
            p23_ref[...] = block[...]
            p1_ref[:, HB:] = block[...]


def relay_kernel(ids, p23_ref, p1_ref, after_ref, q23_ref, q1_ref):
    q23_ref[...] = p23_ref[...]
    q1_ref[...] = p1_ref[...]


def turn_kernel(
    ids, w_ref, y12_ref, y12_in, prior_ref, lh, ll, u3h, u3l, u1h, u1l, u2h, u2l, p23, p23_other, p1, p1_other, *rest
):
    blocks, (y1_ref, y2_ref, y_ref, yb_ref, x_ref, x23_ref, x3_ref, acc) = rest[:6], rest[-8:]
    h = ids[1]
    last = ids[2] == 3
    y1_ref[...] = jnp.where(last, y12_in[0:NB, :], y12_ref[0:NB, :])
    y2 = jnp.where(last, y12_in[NB:, :], y12_ref[NB:, :])
    y2_ref[...] = y2
    acc[...] = w_ref[...]
    block_product(ids, blocks, 1, y1_ref, acc)
    block_product(ids, blocks, 2, y2_ref, acc)
    w = acc[...]
    y3 = w + apply(lh, ll, w)
    y_ref[...] = jnp.where(ids[2] == 3, y3, prior_ref[...])
    yb_ref[...] = y3.astype(BF16)

    def product(same, other, row):
        return dot(same, x_ref[pl.ds(pl.multiple_of(row + h * HB, HB), HB), :]) + dot(
            other, x_ref[pl.ds(pl.multiple_of(row + (1 - h) * HB, HB), HB), :]
        )

    x3 = apply(u3h, u3l, y3).astype(BF16)
    x_ref[2 * NB :, :] = x3
    x23_ref[NB:, :] = x3
    x3_ref[...] = x3
    t = y2.astype(F32) - product(p23[...], p23_other[...], 2 * NB)
    x2 = apply(u2h, u2l, t).astype(BF16)
    x_ref[NB : 2 * NB, :] = x2
    x23_ref[0:NB, :] = x2
    t = y1_ref[...].astype(F32) - product(p1[:, 0:HB], p1_other[:, 0:HB], NB) - product(p1[:, HB:], p1_other[:, HB:], 2 * NB)
    x_ref[0:NB, :] = apply(u1h, u1l, t).astype(BF16)


def hold_kernel(ids, top, bottom, *rest):
    top_out, bottom_out = rest[-2:]
    top_out[...] = top[...]
    bottom_out[...] = bottom[...]


def late_kernel(ids, to0, to1, to2, y1, y2, y3, *rest):
    late_ref, z = rest[-1], ids[2]
    late_ref[0:NB, :] = jnp.where(z >= 1, y1[...], to0[0:NB, :])
    late_ref[NB : 2 * NB, :] = jnp.where(z >= 2, y2[...], to0[NB : 2 * NB, :] + to1[0:NB, :])
    late_ref[2 * NB :, :] = jnp.where(z >= 3, y3[...], to0[2 * NB :, :] + to1[NB:, :] + to2[...])


def unknowns_kernel(ids, v0, e1, e2, e3, late, s1, s2, s3, v_ref, mine_ref, theirs_ref):
    h, owner = ids[1], ids[3] == 0
    v_ref[0:NB, :] = jnp.where(owner, v0[...], e1[...] + e2[...] + e3[...])
    v_ref[NB:, :] = jnp.where(owner, late[...], s1[...] + s2[...] + s3[...])
    for j in range(4):
        rows = slice(j * HB, (j + 1) * HB)
        mine_ref[rows, :] = v_ref[pl.ds(pl.multiple_of(j * NB + h * HB, HB), HB), :]
        theirs_ref[rows, :] = v_ref[pl.ds(pl.multiple_of(j * NB + (1 - h) * HB, HB), HB), :]


def window_kernel(ids, b_ref, v_ref, own_ref, uh_ref, ul_ref, *rest):
    blocks, (out_ref, acc) = rest[:6], rest[6:]
    x, h, z, owner = ids[0], ids[1], ids[2], ids[3] == 0
    acc[...] = jnp.where(owner, own_ref[...], b_ref[...])
    for d in range(NX):
        j = lax.rem(x + d, NX)
        for s in range(2):
            part = h if s == 0 else 1 - h

            @pl.when(jnp.logical_or(jnp.logical_not(owner), j > z))
            def _():
                block = window_blocks(blocks, d)[s]
                acc[...] -= dot(block[...], v_ref[pl.ds(pl.multiple_of(j * NB + part * HB, HB), HB), :])

    @pl.when(owner)
    def _():
        out_ref[...] = apply(uh_ref, ul_ref, acc[...])

    @pl.when(jnp.logical_not(owner))
    def _():
        out_ref[...] = acc[...]


def rows_kernel(tiles, ids, mine_ref, other_ref, *rest):
    blocks, (own_ref, part_ref, v_ref) = rest[:4], rest[4:]
    v_ref[:, 0:128] = mine_ref[...]
    v_ref[:, 128:] = other_ref[...]
    tile = own_ref.shape[0] // tiles
    for t in range(tiles):
        rows = slice(t * tile, (t + 1) * tile)
        total = None
        for d in range(NX):
            j = lax.rem(ids[0] + d, NX)
            term = dot(blocks[d][rows, :], v_ref[pl.ds(pl.multiple_of(j * HB, HB), HB), :])
            total = term if total is None else total + term
        own_ref[rows, :] = total[:, 0:128]
        part_ref[rows, :] = total[:, 128:].astype(BF16)


def add_kernel(ids, out_in, b_ref, own_t, part_t, own_b, part_b, out_ref):
    i, n = pl.program_id(0), out_ref.shape[0]
    half = own_t.shape[0] // n
    for top, own, part in ((True, own_t, part_t), (False, own_b, part_b)):
        @pl.when((i < half) == top)
        def _():
            rows = pl.ds(pl.multiple_of((i if top else i - half) * n, n), n)
            base = b_ref[pl.ds(pl.multiple_of(NB + i * n, 128), n), :]
            out_ref[...] = base - own[rows, :] - part[rows, :].astype(F32)


def whole(shape):
    return pl.BlockSpec(memory_space=pltpu.VMEM)


def in_hbm(a):
    return pltpu.with_memory_space_constraint(a, pltpu.HBM)


ANY = pl.BlockSpec(memory_space=pl.ANY)


def call(kernel, ids, args, specs, outs, scratch=(), grid=(1,), out_spec=None, limit=12, aliases={}):
    out_specs = jax.tree.map(lambda o: whole(o.shape), outs) if out_spec is None else out_spec
    return pl.pallas_call(
        kernel,
        grid_spec=pltpu.PrefetchScalarGridSpec(
            num_scalar_prefetch=1, grid=grid, in_specs=specs, out_specs=out_specs, scratch_shapes=scratch
        ),
        out_shape=outs,
        input_output_aliases=aliases,
        cost_estimate=pl.CostEstimate(flops=1, bytes_accessed=1, transcendentals=0),
        compiler_params=pltpu.CompilerParams(vmem_limit_bytes=limit * 1024 * 1024),
    )(ids, *args)


def body(rhs, factors, diag_inv):
    rows, cols = rhs.shape
    r, c = lax.axis_index("row"), lax.axis_index("col")
    ids = jnp.stack([r // NH, r % NH, c // NY, c % NY]).astype(jnp.int32)

    def bf(n, width=cols):
        return jax.ShapeDtypeStruct((n, width), BF16)

    vec, mat = jax.ShapeDtypeStruct((NB, cols), F32), bf(NB, NB)
    vspec, mspec = whole((NB, cols)), whole((NB, NB))
    first = pl.BlockSpec((NB, cols), lambda i, ids: (0, 0))

    own = factors[:NB]
    same = [own, send(own, x_minus), send(own, x_far), send(own, x_plus)]
    half = (rows - NB) // 2
    own_t, own_b = factors[NB : NB + half], factors[NB + half :]
    own_other = send(own, other_core)
    wspecs = [whole((NB, HB))] * 6

    y_z0, yb0, lh, ll, *uppers = call(
        start_kernel, ids, (in_hbm(rhs), in_hbm(diag_inv), own), [first, pl.BlockSpec((4, NB, NB), lambda i, ids: (0, 0, 0)), ANY],
        (vec, bf(NB), mat, mat) + (mat,) * 6, limit=16,
    )
    hops = [send(yb0, z_move(0, t)) for t in (1, 2, 3)]
    p23, p1, received = call(
        pick_kernel, ids, same, [whole((NB, HB))] * 4, (bf(NB, HB), bf(NB, 2 * HB), bf(3 * NB, HB))
    )
    window = [*same, own_other, send(received, other_core)]
    p23 = send(p23, z_move(2, 3))
    p1 = send(p1, z_move(1, 3))

    def forward(j, w, wspec, own, prior, received, after=()):
        return call(
            functools.partial(forward_kernel, j, len(received)), ids, (w, own, prior, lh, ll, *window, *received, *after),
            [wspec, vspec, vspec, mspec, mspec, *wspecs] + [vspec] * len(received) + [ANY] * len(after), (bf(NB), vec, vec, bf(NB if j == 0 else 2 * NB)),
        )

    y0 = call(combine_kernel, ids, (yb0, *hops), [vspec] * 4, bf(NB))
    early = [send(y0, y_move(t)) for t in (1, 2, 3)]
    top, bottom = call(
        hold_kernel, ids, (own_t, own_b, *early, window[5]), [whole((half, HB))] * 2 + [ANY] * 4, (bf(half, HB),) * 2
    )
    before_t, after_b = send(top, x_plus), send(bottom, x_minus)
    far_t, far_b = send(before_t, x_plus), send(after_b, x_minus)
    _, w0, y_own, yb1 = forward(0, in_hbm(rhs), first, y0, y_z0, ())
    hops = [send(yb1, z_move(1, 2))]
    _, _, y_own, y12 = forward(1, w0, vspec, yb1, y_own, hops)
    y12_in = send(y12, z_move(2, 3))
    p23, p1 = call(relay_kernel, ids, (p23, p1, y12), [whole((NB, HB)), mspec, ANY], (bf(NB, HB), bf(NB, 2 * HB)))
    p23_other, p1_other = send(p23, other_core), send(p1, other_core)
    top, bottom = call(hold_kernel, ids, (own_t, own_b, p23_other), [whole((half, HB))] * 2 + [ANY], (bf(half, HB),) * 2)
    before_b, after_t = send(bottom, x_plus), send(top, x_minus)
    y1, y2, y_own, yb3, xs, x23s, x3s = call(
        turn_kernel, ids,
        (w0, y12, y12_in, y_own, lh, ll, *uppers, p23, p23_other, p1, p1_other, *window, before_t, after_b),
        [vspec] * 4 + [mspec] * 8 + [whole((NB, HB))] * 2 + [mspec] * 2 + wspecs + [ANY] * 2,
        (bf(NB), bf(NB), vec, bf(NB), bf(3 * NB), bf(2 * NB), bf(NB)), scratch=[pltpu.VMEM((NB, cols), F32)],
    )
    to0, to1, to2 = send(xs, z_move(3, 0)), send(x23s, z_move(3, 1)), send(x3s, z_move(3, 2))
    late = call(
        late_kernel, ids, (to0, to1, to2, y1, y2, yb3, before_b, after_t),
        [whole((3 * NB, cols)), whole((2 * NB, cols))] + [vspec] * 4 + [ANY] * 2, bf(3 * NB),
    )
    spread = [send(late, y_move(t)) for t in (1, 2, 3)]
    out = jax.ShapeDtypeStruct((rows, cols), F32)
    v, mine, theirs = call(
        unknowns_kernel, ids, (y0, *early, late, *spread), [vspec] * 4 + [whole((3 * NB, cols))] * 4,
        (bf(4 * NB), bf(4 * HB), bf(4 * HB)),
    )
    other = send(theirs, other_core)
    done = call(
        window_kernel, ids, (in_hbm(rhs), v, y_own, uppers[0], uppers[1], *window),
        [first, whole((4 * NB, cols)), vspec, mspec, mspec, *wspecs], out, out_spec=first, scratch=[pltpu.VMEM((NB, cols), F32)],
    )
    sums, parts = [], []
    for blocks in ((own_t, after_t, far_t, before_t), (own_b, after_b, far_b, before_b)):
        total, part = call(
            functools.partial(rows_kernel, 2), ids, (mine, other, *blocks),
            [vspec] * 2 + [mspec] * 4, (jax.ShapeDtypeStruct((half, cols), F32), bf(half)),
            scratch=[pltpu.VMEM((4 * HB, 2 * cols), BF16)], limit=24,
        )
        sums.append(total)
        parts.append(send(part, other_core))
    tile = half // 2
    at = pl.BlockSpec((pl.Element(tile), pl.Element(cols)), lambda i, ids: (pl.multiple_of(NB + i * tile, 128), 0))
    return call(
        add_kernel, ids, (done, rhs, sums[0], parts[0], sums[1], parts[1]),
        [ANY] + [vspec] * 5, out, grid=(4,), out_spec=at, aliases={1: 0},
    )


def solution(mesh):
    placed = (P("col", "row"), P("col", "row"), P())
    return jax.shard_map(body, mesh=mesh, in_specs=placed, out_specs=P("col", "row"), check_vma=False)
```

```python
import functools

import jax
import jax.numpy as jnp
from jax import lax
from jax.experimental import pallas as pl
from jax.experimental.pallas import tpu as pltpu
from jax.sharding import PartitionSpec as P

NX, NH, NZ, NY = 4, 2, 4, 4
NB = 512
HB = 256
F32, BF16 = jnp.float32, jnp.bfloat16


def pairs(move):
    out = []
    for r in range(NX * NH):
        for c in range(NZ * NY):
            x, h = divmod(r, NH)
            z, y = divmod(c, NY)
            to = move(x, h, z, y)
            if to is not None:
                x2, h2, z2, y2 = to
                out.append((r * NZ * NY + c, ((x2 % NX) * NH + h2 % NH) * NZ * NY + (z2 % NZ) * NY + y2 % NY))
    return out


def send(value, move):
    return lax.ppermute(value, ("row", "col"), pairs(move))


def x_plus(x, h, z, y):
    return (x + 1, h, z, y)


def x_minus(x, h, z, y):
    return (x - 1, h, z, y)


def x_far(x, h, z, y):
    return (x + 2, h, z, y)


def other_core(x, h, z, y):
    return (x, 1 - h, z, y)


def z_move(src, dst):
    return lambda x, h, z, y: (x, h, dst, y) if (y == 0 and z == src) else None


def y_move(step):
    return lambda x, h, z, y: (x, h, z, step) if y == 0 else None


def dot(a, b):
    return jnp.dot(a, b, preferred_element_type=F32)


def split(a):
    hi = a.astype(BF16)
    return hi, (a - hi.astype(F32)).astype(BF16)


def apply(hi_ref, lo_ref, v):
    vh, vl = split(v)
    wide = dot(hi_ref[...], jnp.concatenate([vh, vl], axis=1))
    return wide[:, 0:128] + (wide[:, 128:] + dot(lo_ref[...], vh))


def apply_high(hi_ref, v):
    vh, vl = split(v)
    wide = dot(hi_ref[...], jnp.concatenate([vh, vl], axis=1))
    return wide[:, 0:128] + wide[:, 128:]


def lower_mask(d):
    i = lax.broadcasted_iota(jnp.int32, d.shape, 0)
    j = lax.broadcasted_iota(jnp.int32, d.shape, 1)
    return jnp.where(i > j, d, 0.0)


def upper_mask(d):
    i = lax.broadcasted_iota(jnp.int32, d.shape, 0)
    j = lax.broadcasted_iota(jnp.int32, d.shape, 1)
    return jnp.where(i <= j, d, 0.0)


def start_kernel(ids, b_ref, d_ref, after_ref, y_ref, yb_ref, lh_ref, ll_ref, *uppers):
    lh_ref[...], ll_ref[...] = split(lower_mask(d_ref[ids[2]]))
    w = b_ref[...]
    y = w + apply(lh_ref, ll_ref, w)
    y_ref[...] = y
    yb_ref[...] = y.astype(BF16)
    for n, j in enumerate((ids[2], 1, 2)):
        uppers[2 * n][...], uppers[2 * n + 1][...] = split(upper_mask(d_ref[j]))


def combine_kernel(ids, own_ref, r1, r2, r3, v_ref):
    v_ref[...] = own_or_received(ids, 0, own_ref, (r1, r2, r3))


def own_or_received(ids, j, own_ref, received):
    if not received:
        return own_ref[...]
    total = received[0][...]
    for piece in received[1:]:
        total = total + piece[...]
    return jnp.where(ids[2] == j, own_ref[...], total)


def window_blocks(blocks, d):
    return blocks[d], (blocks[4] if d == 0 else blocks[5].at[(d - 1) * NB : d * NB, :])


def block_product(ids, blocks, j, v_ref, acc_ref):
    x, h = ids[0], ids[1]
    for d in range(NX):
        @pl.when(lax.rem(x + d, NX) == j)
        def _():
            same, other = window_blocks(blocks, d)
            acc_ref[...] -= dot(same[...], v_ref[pl.ds(pl.multiple_of(h * HB, HB), HB), :]) + dot(
                other[...], v_ref[pl.ds(pl.multiple_of((1 - h) * HB, HB), HB), :]
            )


def forward_kernel(j, count, ids, w_ref, own_ref, prior_ref, lh_ref, ll_ref, *rest):
    blocks, received, (v_ref, w_out, y_ref, yb_ref) = rest[:6], rest[6 : 6 + count], rest[-4:]
    v_ref[...] = own_or_received(ids, j, own_ref, received)
    w_out[...] = w_ref[...]
    block_product(ids, blocks, j, v_ref, w_out)
    w = w_out[...]
    y = w + apply_high(lh_ref, w)
    y_ref[...] = jnp.where(ids[2] == j + 1, y, prior_ref[...])
    if j == 0:
        yb_ref[...] = y.astype(BF16)
    else:
        yb_ref[0:NB, :] = v_ref[...]
        yb_ref[NB:, :] = y.astype(BF16)


def pick_kernel(ids, b0, b1, b2, b3, p23_ref, p1_ref, all_ref):
    for d, block in enumerate((b1, b2, b3)):
        all_ref[d * NB : (d + 1) * NB, :] = block[...]
    for d, block in enumerate((b0, b1, b2, b3)):
        @pl.when(lax.rem(ids[0] + d, NX) == 2)
        def _():
            p1_ref[:, 0:HB] = block[...]

        @pl.when(lax.rem(ids[0] + d, NX) == 3)
        def _():
            p23_ref[...] = block[...]
            p1_ref[:, HB:] = block[...]


def relay_kernel(ids, p23_ref, p1_ref, after_ref, q23_ref, q1_ref):
    q23_ref[...] = p23_ref[...]
    q1_ref[...] = p1_ref[...]


def turn_kernel(
    ids, w_ref, y12_ref, y12_in, prior_ref, lh, ll, u3h, u3l, u1h, u1l, u2h, u2l, p23, p23_other, p1, p1_other, *rest
):
    blocks, (y1_ref, y2_ref, y_ref, yb_ref, x_ref, x23_ref, x3_ref, acc) = rest[:6], rest[-8:]
    h = ids[1]
    last = ids[2] == 3
    y1_ref[...] = jnp.where(last, y12_in[0:NB, :], y12_ref[0:NB, :])
    y2 = jnp.where(last, y12_in[NB:, :], y12_ref[NB:, :])
    y2_ref[...] = y2
    acc[...] = w_ref[...]
    block_product(ids, blocks, 1, y1_ref, acc)
    block_product(ids, blocks, 2, y2_ref, acc)
    w = acc[...]
    y3 = w + apply_high(lh, w)
    y_ref[...] = jnp.where(ids[2] == 3, y3, prior_ref[...])
    yb_ref[...] = y3.astype(BF16)

    def product(same, other, row):
        return dot(same, x_ref[pl.ds(pl.multiple_of(row + h * HB, HB), HB), :]) + dot(
            other, x_ref[pl.ds(pl.multiple_of(row + (1 - h) * HB, HB), HB), :]
        )

    x3 = apply_high(u3h, y3).astype(BF16)
    x_ref[2 * NB :, :] = x3
    x23_ref[NB:, :] = x3
    x3_ref[...] = x3
    t = y2.astype(F32) - product(p23[...], p23_other[...], 2 * NB)
    x2 = apply_high(u2h, t).astype(BF16)
    x_ref[NB : 2 * NB, :] = x2
    x23_ref[0:NB, :] = x2
    t = y1_ref[...].astype(F32) - product(p1[:, 0:HB], p1_other[:, 0:HB], NB) - product(p1[:, HB:], p1_other[:, HB:], 2 * NB)
    x_ref[0:NB, :] = apply_high(u1h, t).astype(BF16)


def hold_kernel(ids, top, bottom, *rest):
    top_out, bottom_out = rest[-2:]
    top_out[...] = top[...]
    bottom_out[...] = bottom[...]


def late_kernel(ids, to0, to1, to2, y1, y2, y3, *rest):
    late_ref, z = rest[-1], ids[2]
    late_ref[0:NB, :] = jnp.where(z >= 1, y1[...], to0[0:NB, :])
    late_ref[NB : 2 * NB, :] = jnp.where(z >= 2, y2[...], to0[NB : 2 * NB, :] + to1[0:NB, :])
    late_ref[2 * NB :, :] = jnp.where(z >= 3, y3[...], to0[2 * NB :, :] + to1[NB:, :] + to2[...])


def unknowns_kernel(ids, v0, e1, e2, e3, late, s1, s2, s3, v_ref, mine_ref, theirs_ref):
    h, owner = ids[1], ids[3] == 0
    v_ref[0:NB, :] = jnp.where(owner, v0[...], e1[...] + e2[...] + e3[...])
    v_ref[NB:, :] = jnp.where(owner, late[...], s1[...] + s2[...] + s3[...])
    for j in range(4):
        rows = slice(j * HB, (j + 1) * HB)
        mine_ref[rows, :] = v_ref[pl.ds(pl.multiple_of(j * NB + h * HB, HB), HB), :]
        theirs_ref[rows, :] = v_ref[pl.ds(pl.multiple_of(j * NB + (1 - h) * HB, HB), HB), :]


def window_kernel(ids, b_ref, v_ref, own_ref, uh_ref, ul_ref, *rest):
    blocks, (out_ref, acc) = rest[:6], rest[6:]
    x, h, z, owner = ids[0], ids[1], ids[2], ids[3] == 0
    acc[...] = jnp.where(owner, own_ref[...], b_ref[...])
    for d in range(NX):
        j = lax.rem(x + d, NX)
        for s in range(2):
            part = h if s == 0 else 1 - h

            @pl.when(jnp.logical_or(jnp.logical_not(owner), j > z))
            def _():
                block = window_blocks(blocks, d)[s]
                acc[...] -= dot(block[...], v_ref[pl.ds(pl.multiple_of(j * NB + part * HB, HB), HB), :])

    @pl.when(owner)
    def _():
        out_ref[...] = apply(uh_ref, ul_ref, acc[...])

    @pl.when(jnp.logical_not(owner))
    def _():
        out_ref[...] = acc[...]


def rows_kernel(tiles, ids, mine_ref, other_ref, *rest):
    blocks, (own_ref, part_ref, v_ref) = rest[:4], rest[4:]
    v_ref[:, 0:128] = mine_ref[...]
    v_ref[:, 128:] = other_ref[...]
    tile = own_ref.shape[0] // tiles
    for t in range(tiles):
        rows = slice(t * tile, (t + 1) * tile)
        total = None
        for d in range(NX):
            j = lax.rem(ids[0] + d, NX)
            term = dot(blocks[d][rows, :], v_ref[pl.ds(pl.multiple_of(j * HB, HB), HB), :])
            total = term if total is None else total + term
        own_ref[rows, :] = total[:, 0:128]
        part_ref[rows, :] = total[:, 128:].astype(BF16)


def add_kernel(ids, out_in, b_ref, own_t, part_t, own_b, part_b, out_ref):
    i, n = pl.program_id(0), out_ref.shape[0]
    half = own_t.shape[0] // n
    for top, own, part in ((True, own_t, part_t), (False, own_b, part_b)):
        @pl.when((i < half) == top)
        def _():
            rows = pl.ds(pl.multiple_of((i if top else i - half) * n, n), n)
            base = b_ref[pl.ds(pl.multiple_of(NB + i * n, 128), n), :]
            out_ref[...] = base - own[rows, :] - part[rows, :].astype(F32)


def whole(shape):
    return pl.BlockSpec(memory_space=pltpu.VMEM)


def in_hbm(a):
    return pltpu.with_memory_space_constraint(a, pltpu.HBM)


ANY = pl.BlockSpec(memory_space=pl.ANY)


def call(kernel, ids, args, specs, outs, scratch=(), grid=(1,), out_spec=None, limit=12, aliases={}):
    out_specs = jax.tree.map(lambda o: whole(o.shape), outs) if out_spec is None else out_spec
    return pl.pallas_call(
        kernel,
        grid_spec=pltpu.PrefetchScalarGridSpec(
            num_scalar_prefetch=1, grid=grid, in_specs=specs, out_specs=out_specs, scratch_shapes=scratch
        ),
        out_shape=outs,
        input_output_aliases=aliases,
        cost_estimate=pl.CostEstimate(flops=1, bytes_accessed=1, transcendentals=0),
        compiler_params=pltpu.CompilerParams(vmem_limit_bytes=limit * 1024 * 1024),
    )(ids, *args)


def body(rhs, factors, diag_inv):
    rows, cols = rhs.shape
    r, c = lax.axis_index("row"), lax.axis_index("col")
    ids = jnp.stack([r // NH, r % NH, c // NY, c % NY]).astype(jnp.int32)

    def bf(n, width=cols):
        return jax.ShapeDtypeStruct((n, width), BF16)

    vec, mat = jax.ShapeDtypeStruct((NB, cols), F32), bf(NB, NB)
    vspec, mspec = whole((NB, cols)), whole((NB, NB))
    first = pl.BlockSpec((NB, cols), lambda i, ids: (0, 0))

    own = factors[:NB]
    same = [own, send(own, x_minus), send(own, x_far), send(own, x_plus)]
    half = (rows - NB) // 2
    own_t, own_b = factors[NB : NB + half], factors[NB + half :]
    own_other = send(own, other_core)
    wspecs = [whole((NB, HB))] * 6

    y_z0, yb0, lh, ll, *uppers = call(
        start_kernel, ids, (in_hbm(rhs), in_hbm(diag_inv), own), [first, pl.BlockSpec((4, NB, NB), lambda i, ids: (0, 0, 0)), ANY],
        (vec, bf(NB), mat, mat) + (mat,) * 6, limit=16,
    )
    hops = [send(yb0, z_move(0, t)) for t in (1, 2, 3)]
    p23, p1, received = call(
        pick_kernel, ids, same, [whole((NB, HB))] * 4, (bf(NB, HB), bf(NB, 2 * HB), bf(3 * NB, HB))
    )
    window = [*same, own_other, send(received, other_core)]
    p23 = send(p23, z_move(2, 3))
    p1 = send(p1, z_move(1, 3))

    def forward(j, w, wspec, own, prior, received, after=()):
        return call(
            functools.partial(forward_kernel, j, len(received)), ids, (w, own, prior, lh, ll, *window, *received, *after),
            [wspec, vspec, vspec, mspec, mspec, *wspecs] + [vspec] * len(received) + [ANY] * len(after), (bf(NB), vec, vec, bf(NB if j == 0 else 2 * NB)),
        )

    y0 = call(combine_kernel, ids, (yb0, *hops), [vspec] * 4, bf(NB))
    early = [send(y0, y_move(t)) for t in (1, 2, 3)]
    top, bottom = call(
        hold_kernel, ids, (own_t, own_b, *early, window[5]), [whole((half, HB))] * 2 + [ANY] * 4, (bf(half, HB),) * 2
    )
    before_t, after_b = send(top, x_plus), send(bottom, x_minus)
    far_t, far_b = send(before_t, x_plus), send(after_b, x_minus)
    _, w0, y_own, yb1 = forward(0, in_hbm(rhs), first, y0, y_z0, ())
    hops = [send(yb1, z_move(1, 2))]
    _, _, y_own, y12 = forward(1, w0, vspec, yb1, y_own, hops)
    y12_in = send(y12, z_move(2, 3))
    top, bottom = call(hold_kernel, ids, (own_t, own_b, y12_in), [whole((half, HB))] * 2 + [ANY], (bf(half, HB),) * 2)
    before_b, after_t = send(bottom, x_plus), send(top, x_minus)
    p23, p1 = call(relay_kernel, ids, (p23, p1, y12), [whole((NB, HB)), mspec, ANY], (bf(NB, HB), bf(NB, 2 * HB)))
    p23_other, p1_other = send(p23, other_core), send(p1, other_core)
    y1, y2, y_own, yb3, xs, x23s, x3s = call(
        turn_kernel, ids,
        (w0, y12, y12_in, y_own, lh, ll, *uppers, p23, p23_other, p1, p1_other, *window, before_t, after_b),
        [vspec] * 4 + [mspec] * 8 + [whole((NB, HB))] * 2 + [mspec] * 2 + wspecs + [ANY] * 2,
        (bf(NB), bf(NB), vec, bf(NB), bf(3 * NB), bf(2 * NB), bf(NB)), scratch=[pltpu.VMEM((NB, cols), F32)],
    )
    to0, to1, to2 = send(xs, z_move(3, 0)), send(x23s, z_move(3, 1)), send(x3s, z_move(3, 2))
    late = call(
        late_kernel, ids, (to0, to1, to2, y1, y2, yb3, before_b, after_t),
        [whole((3 * NB, cols)), whole((2 * NB, cols))] + [vspec] * 4 + [ANY] * 2, bf(3 * NB),
    )
    spread = [send(late, y_move(t)) for t in (1, 2, 3)]
    out = jax.ShapeDtypeStruct((rows, cols), F32)
    v, mine, theirs = call(
        unknowns_kernel, ids, (y0, *early, late, *spread), [vspec] * 4 + [whole((3 * NB, cols))] * 4,
        (bf(4 * NB), bf(4 * HB), bf(4 * HB)),
    )
    other = send(theirs, other_core)
    done = call(
        window_kernel, ids, (in_hbm(rhs), v, y_own, uppers[0], uppers[1], *window),
        [first, whole((4 * NB, cols)), vspec, mspec, mspec, *wspecs], out, out_spec=first, scratch=[pltpu.VMEM((NB, cols), F32)],
    )
    sums, parts = [], []
    for blocks in ((own_t, after_t, far_t, before_t), (own_b, after_b, far_b, before_b)):
        total, part = call(
            functools.partial(rows_kernel, 2), ids, (mine, other, *blocks),
            [vspec] * 2 + [mspec] * 4, (jax.ShapeDtypeStruct((half, cols), F32), bf(half)),
            scratch=[pltpu.VMEM((4 * HB, 2 * cols), BF16)], limit=24,
        )
        sums.append(total)
        parts.append(send(part, other_core))
    tile = half // 2
    at = pl.BlockSpec((pl.Element(tile), pl.Element(cols)), lambda i, ids: (pl.multiple_of(NB + i * tile, 128), 0))
    return call(
        add_kernel, ids, (done, rhs, sums[0], parts[0], sums[1], parts[1]),
        [ANY] + [vspec] * 5, out, grid=(4,), out_spec=at, aliases={1: 0},
    )


def solution(mesh):
    placed = (P("col", "row"), P("col", "row"), P())
    return jax.shard_map(body, mesh=mesh, in_specs=placed, out_specs=P("col", "row"), check_vma=False)
```
